256 devices in a mesh: req: 64 (over x_lo, y, z), ctx: 4 (over x_hi, core).
Axes of the slice: x: 4 (x_hi: 2, x_lo: 2; x = x_hi * 2 + x_lo), y: 4, z: 8, core: 2. Of those that a mesh axis runs over, the one named last changes fastest.
Arguments:
- q_nope: bfloat16 [64, 128, 8192], P('req'), may hold values from -6 to 6
- q_rope: bfloat16 [64, 128, 4096], P('req'), may hold values from -600 to 600
- cache_latent: bfloat16 [64, 1024, 512], P('req', 'ctx'), may hold values from -6 to 6
- cache_rope: bfloat16 [64, 1024, 64], P('req', 'ctx'), may hold values from -4 to 4
- new_latent: bfloat16 [64, 128, 512], P('req', 'ctx'), may hold values from -6 to 6
- new_rope: bfloat16 [64, 128, 64], P('req', 'ctx'), may hold values from -8 to 8
- lengths: int32 [64, 4], P('req', 'ctx'), may hold values from 64 to 256, as said below
- w_key: bfloat16 [512, 8192], P(None, 'ctx'), may hold values from -0.25 to 0.25
- w_value: bfloat16 [512, 8192], P(None, 'ctx'), may hold values from -0.25 to 0.25
Outputs:
- attended: bfloat16 [64, 128, 8192], P('req', None, 'ctx')
The draws below stay inside these ranges and needn't reach their ends.
Inputs may be any that keep to these rules, and one draw needn't show every extreme that they name: lengths[r, g] counts the live cached rows at the start of request r's slots in context group g; all cached rows precede the new tokens; some entry equals 256 in every draw.
All inputs are finite; a program needn't handle non-finite values.
Results may differ from the reference program's by a relative error of at most 0.015.
Values may be sent and summed in bfloat16 or wider, within the bound.
A program may use at most 128 MiB of HBM per device.

```python
import math
import jax
import jax.numpy as jnp
from jax import lax

DC = 512
DR = 64
DH = 128
DV = 128
HEADS = 64
Q_NEW = 128
ROWS_DEV = 256
REQS = 64
CTX_ROWS = 1024
N_CTX = 4


def rope_pair(key):
    base_key = jax.random.fold_in(key, 4242)
    key_query, key_fresh = jax.random.split(base_key, 2)
    query_draw = jnp.clip(jax.random.normal(key_query, (REQS, Q_NEW, HEADS * DR), jnp.float32), -4.0, 4.0)
    fresh_draw = jnp.clip(jax.random.normal(key_fresh, (REQS, Q_NEW, DR), jnp.float32), -4.0, 4.0)
    return (query_draw, fresh_draw)


def draw_q_rope(key, part):
    query_draw, fresh_draw = rope_pair(key)
    return query_draw.astype(jnp.bfloat16)


def draw_new_rope(key, part):
    query_draw, fresh_draw = rope_pair(key)
    return fresh_draw.astype(jnp.bfloat16)


def draw_lengths(key, part):
    key_draw, key_pick = jax.random.split(jax.random.fold_in(key, 31), 2)
    grid_shape = (REQS, N_CTX)
    lengths_flat = jax.random.randint(key_draw, grid_shape, ROWS_DEV // 4, ROWS_DEV + 1).reshape(-1)
    chosen = jax.random.randint(key_pick, (), 0, REQS * N_CTX)
    lengths_flat = jnp.where(jnp.arange(REQS * N_CTX) == chosen, ROWS_DEV, lengths_flat)
    return lengths_flat.reshape(grid_shape).astype(jnp.int32)


def level_of(key, extent, cuts, least, high):
    def one(dim, shards_of):
        heights = jax.random.uniform(jax.random.fold_in(jax.random.fold_in(key, 6), dim), (shards_of,), jnp.float32, least / len(cuts), high / len(cuts))
        return jnp.repeat(jnp.exp(heights), extent[dim] // shards_of).reshape((-1,) + (1,) * (len(extent) - dim - 1))

    loudness = one(*cuts[0])
    for cut in cuts[1:]:
        loudness = loudness * one(*cut)
    return loudness


def gaussian(key, shape, scale, limit, cuts=(), kind=jnp.bfloat16):
    factor_of = level_of(key, shape, cuts, -0.22, 0.18) if cuts else 1.0
    entries = jax.random.normal(key, shape, jnp.float32) * scale * factor_of
    return jnp.minimum(jnp.maximum(entries, -limit), limit).astype(kind)


def setup_inputs(seed: int = 0) -> dict:
    seeds = jax.random.split(jax.random.key(seed), 10)
    q_nope = gaussian(seeds[0], (REQS, Q_NEW, HEADS * DH), 1.0, 6.0, ((0, 64),))
    q_rope = draw_q_rope(jax.random.fold_in(seeds[9], 71), 0)
    cache_latent = gaussian(seeds[2], (REQS, CTX_ROWS, DC), 1.0, 6.0, ((0, 64), (1, 4)))
    cache_rope = gaussian(seeds[3], (REQS, CTX_ROWS, DR), 1.0, 4.0, ((0, 64), (1, 4)))
    new_latent = gaussian(seeds[4], (REQS, Q_NEW, DC), 1.0, 6.0, ((0, 64), (1, 4)))
    new_rope = draw_new_rope(jax.random.fold_in(seeds[9], 71), 0)
    lengths = draw_lengths(jax.random.fold_in(seeds[9], 71), 0)
    w_key = gaussian(seeds[7], (DC, HEADS * DH), DC ** -0.5, 0.25, ((1, 4),))
    w_value = gaussian(seeds[8], (DC, HEADS * DV), DC ** -0.5, 0.25, ((1, 4),))
    return {"q_nope": q_nope, "q_rope": q_rope, "cache_latent": cache_latent, "cache_rope": cache_rope, "new_latent": new_latent, "new_rope": new_rope, "lengths": lengths, "w_key": w_key, "w_value": w_value}


blocked_score = -1e+30

def reference(q_nope, q_rope, cache_latent, cache_rope, new_latent, new_rope, lengths, w_key, w_value):
    score_scale = 1.0 / math.sqrt(DH + DR)
    cached_count = ROWS_DEV * N_CTX
    local_rows = jnp.arange(cached_count, dtype=jnp.int32) % ROWS_DEV
    query_rows = jnp.arange(Q_NEW, dtype=jnp.int32)
    causal = query_rows[None, :] <= query_rows[:, None]

    def per_request(request_item):
        query_nope, query_rope, cache_rows, cache_keys, fresh_rows, fresh_keys, live_rows = request_item
        latent = jnp.concatenate([cache_rows, fresh_rows], axis=0)
        rope_keys = jnp.concatenate([cache_keys, fresh_keys], axis=0)
        total_rows = latent.shape[0]
        key_rows = jnp.dot(latent, w_key, preferred_element_type=jnp.float32).astype(jnp.bfloat16)
        value_rows = jnp.dot(latent, w_value, preferred_element_type=jnp.float32).astype(jnp.bfloat16)
        key_rows = lax.optimization_barrier(key_rows).astype(jnp.float32).reshape(total_rows, HEADS, DH)
        value_rows = lax.optimization_barrier(value_rows).astype(jnp.float32).reshape(total_rows, HEADS, DV)
        cached_ok = local_rows < jnp.repeat(live_rows, ROWS_DEV)
        visible = jnp.concatenate([jnp.broadcast_to(cached_ok[None, :], (Q_NEW, cached_count)), causal], axis=1)
        nope_part = query_nope.astype(jnp.float32).reshape(Q_NEW, HEADS, DH)
        rope_part = query_rope.astype(jnp.float32).reshape(Q_NEW, HEADS, DR)
        scores = jnp.einsum('qhd,khd->qhk', nope_part, key_rows)
        scores = scores + jnp.einsum('qhd,kd->qhk', rope_part, rope_keys.astype(jnp.float32))
        scores = jnp.where(visible[:, None, :], scores * score_scale, blocked_score)
        row_level = lax.optimization_barrier(jnp.max(scores, axis=-1, keepdims=True))
        weights = jnp.where(visible[:, None, :], jnp.exp(scores - row_level), 0.0)
        weight_sum = lax.optimization_barrier(jnp.sum(weights, axis=-1))
        rounded = lax.optimization_barrier(weights.astype(jnp.bfloat16)).astype(jnp.float32)
        numerator = jnp.einsum('qhk,khd->qhd', rounded, value_rows)
        return (numerator / weight_sum[..., None]).reshape(Q_NEW, HEADS * DV).astype(jnp.bfloat16)
    return lax.map(per_request, (q_nope, q_rope, cache_latent, cache_rope, new_latent, new_rope, lengths))
```

```python
import functools
import math

import jax
import jax.numpy as jnp
from jax import lax
from jax.experimental import pallas as pl
from jax.experimental.pallas import tpu as pltpu
from jax.sharding import PartitionSpec as P

DC = 512
DR = 64
DH = 128
DV = 128
HEADS = 64
CTX = 4
HERE = HEADS // CTX
PAIRS = HERE // 2
Q = 128
ROWS = 256
NEW = 32
HALF = ROWS // 2
NROW = CTX * (ROWS + NEW)
KEXT = DC + 128
LOG2E = 1.4426950408889634
SCALE = LOG2E / math.sqrt(DH + DR)
BLOCKED = -1e30
MESH = pl.DeviceIdType.MESH
F32 = jnp.float32
BF16 = jnp.bfloat16

NEW0 = CTX * ROWS
SLOT_ROWS = (
    ((0, 0, ROWS),),
    ((ROWS, 0, ROWS),),
    ((2 * ROWS, 0, HALF), (3 * ROWS, HALF, HALF)),
    ((2 * ROWS + HALF, 0, HALF), (3 * ROWS + HALF, HALF, HALF)),
)


def kernel(
    qn_hbm, qr_hbm, cl_hbm, cr_hbm, nl_hbm, nr_hbm, len_hbm, wk_hbm, wv_hbm, o_hbm,
    qn, qr, wk, wv, lat, rope, nrope, lens, ext, latt, qt, acc, top, total, out,
    load_sem, out_sem, sib_send, sib_recv, par_send, par_recv, fwd_send, fwd_recv,
):
    me = lax.axis_index("ctx")
    sib = me + 1 - 2 * lax.rem(me, 2)
    par = lax.rem(me + 2, CTX)
    far = lax.rem(sib + 2, CTX)

    def local(index, src, dst):
        return pltpu.make_async_copy(src, dst, load_sem.at[index])

    loads = dict(
        wk=local(0, wk_hbm, wk),
        qn=local(1, qn_hbm.at[0, :, pl.ds(pl.multiple_of(me * HERE * DH, HERE * DH), HERE * DH)], qn),
        qr=local(2, qr_hbm.at[0, :, pl.ds(pl.multiple_of(me * HERE * DR, HERE * DR), HERE * DR)], qr),
        cl=local(3, cl_hbm.at[0], lat.at[pl.ds(0, ROWS)]),
        cr=local(4, cr_hbm.at[0], rope.at[0]),
        nl=local(5, nl_hbm.at[0], lat.at[pl.ds(NEW0, NEW)]),
        nr=local(6, nr_hbm.at[0], nrope.at[0]),
        ln=local(7, len_hbm, lens.at[0]),
        wv=local(8, wv_hbm, wv),
    )
    barrier = pltpu.get_barrier_semaphore()
    for peer in (sib, par):
        pl.semaphore_signal(barrier, inc=1, device_id={"ctx": peer}, device_id_type=MESH)
    for name in ("wk", "qn", "qr", "cl", "cr", "nl", "nr", "ln", "wv"):
        loads[name].start()
    pl.semaphore_wait(barrier, 2)

    def remote(src, dst, send, recv, index, peer):
        return pltpu.make_async_remote_copy(
            src_ref=src, dst_ref=dst, send_sem=send.at[index], recv_sem=recv.at[index],
            device_id={"ctx": peer}, device_id_type=MESH,
        )

    def small(slot):
        return (
            rope.at[slot], lens.at[slot], nrope.at[slot], lat.at[pl.ds(NEW0 + slot * NEW, NEW)],
        )

    mine = (cr_hbm.at[0], len_hbm, nr_hbm.at[0], nl_hbm.at[0])
    halves = tuple(cl_hbm.at[0, pl.ds(HALF * k, HALF)] for k in range(2))

    def landed(slot):
        return tuple(lat.at[pl.ds(row, count)] for row, _, count in SLOT_ROWS[slot])

    to_par = [
        remote(src, dst, par_send, par_recv, k, par)
        for k, (src, dst) in enumerate(zip(mine + halves, small(2) + landed(2)))
    ]
    to_sib = [
        remote(src, dst, sib_send, sib_recv, k, sib)
        for k, (src, dst) in enumerate(zip(mine + (cl_hbm.at[0],), small(1) + landed(1)))
    ]
    forward = [
        remote(src, dst, fwd_send, fwd_recv, k, sib)
        for k, (src, dst) in enumerate(zip(small(2) + landed(2), small(3) + landed(3)))
    ]
    for copy in to_par + to_sib:
        copy.start()

    top[...] = jnp.full_like(top, BLOCKED)
    total[...] = jnp.zeros_like(total)
    acc[...] = jnp.zeros_like(acc)
    row_of = lax.broadcasted_iota(jnp.int32, (KEXT - DC - DR, 2 * Q), 0)
    tail = jnp.where(row_of == 0, BLOCKED, 0.0).astype(BF16)
    for pair in range(PAIRS):
        qt[pair, DC + DR :, :] = tail

    loads["wk"].wait()
    loads["qn"].wait()
    loads["qr"].wait()
    for head in range(HERE):
        pair, side = head // 2, (head % 2) * Q
        part = lax.dot_general(
            wk[:, head * DH : (head + 1) * DH], qn[:, head * DH : (head + 1) * DH],
            (((1,), (1,)), ((), ())), preferred_element_type=F32,
        )
        qt[pair, :DC, side : side + Q] = part.astype(BF16)
    for pair in range(PAIRS):
        turned = qr[:, pair * 2 * DR : (pair + 1) * 2 * DR].T
        qt[pair, DC : DC + DR, :Q] = turned[:DR]
        qt[pair, DC : DC + DR, Q:] = turned[DR:]

    lane = lax.broadcasted_iota(jnp.int32, (ROWS, KEXT - DC), 1)
    row = lax.broadcasted_iota(jnp.int32, (ROWS, KEXT - DC), 0)

    def widen(rotary, live):
        padded = jnp.concatenate([rotary, jnp.zeros_like(rotary)], axis=1).astype(F32)
        if live is not None:
            padded = jnp.where((lane == DR) & (row >= live), 1.0, padded)
        return padded.astype(BF16)

    def prepare_small(slot):
        wide = widen(rope[slot], jnp.broadcast_to(lens[slot], (ROWS, KEXT - DC)))
        for begin, first, count in SLOT_ROWS[slot]:
            ext[begin : begin + count, :] = wide[first : first + count]
        begin = NEW0 + slot * NEW
        ext[begin : begin + NEW, :] = widen(nrope[slot], None)

    def turn(begin, count):
        latt[:, begin : begin + count] = lat[begin : begin + count, :].T

    def step(pair, begin, count, fresh):
        keys = jnp.concatenate(
            [lat[begin : begin + count, :], ext[begin : begin + count, :]], axis=1
        )
        scores = jnp.dot(keys, qt[pair], preferred_element_type=F32)
        if fresh is not None:
            scores = jnp.concatenate(
                [scores[: NEW0 - begin], jnp.where(fresh, scores[NEW0 - begin :], BLOCKED)], axis=0
            )
        old = top[pair]
        level = jnp.maximum(old, jnp.max(scores, axis=0, keepdims=True))
        factor = jnp.exp2((old - level) * SCALE)
        weights = jnp.exp2((scores - level) * SCALE)
        top[pair] = level
        total[pair] = total[pair] * factor + jnp.sum(weights, axis=0, keepdims=True)
        acc[pair] = acc[pair] * factor + jnp.dot(
            latt[:, begin : begin + count], weights.astype(BF16), preferred_element_type=F32
        )

    def steps(first, last, begin, count, fresh=None):
        def body(pair, carry):
            step(pair, begin, count, fresh)
            return carry

        lax.fori_loop(first, last, body, 0, unroll=2)

    for name in ("cl", "cr", "nl", "nr", "ln"):
        loads[name].wait()
    for copy in to_sib:
        copy.wait_recv()
    prepare_small(0)
    prepare_small(1)
    turn(0, 2 * ROWS)
    steps(0, PAIRS // 2, 0, 2 * ROWS)
    for arrived, onward in zip(to_par[:5], forward[:5]):
        arrived.wait_recv()
        onward.start()
    prepare_small(2)
    turn(2 * ROWS, HALF)
    steps(PAIRS // 2, PAIRS, 0, 2 * ROWS)
    for copy in forward[:5]:
        copy.wait_recv()
    prepare_small(3)
    turn(2 * ROWS + HALF, HALF)
    steps(0, PAIRS // 2, 2 * ROWS, ROWS)
    to_par[5].wait_recv()
    forward[5].start()
    steps(PAIRS // 2, PAIRS, 2 * ROWS, ROWS)
    forward[5].wait_recv()
    turn(3 * ROWS, ROWS + CTX * NEW)
    local_row = lax.broadcasted_iota(jnp.int32, (CTX * NEW, 2 * Q), 0)
    query = lax.rem(lax.broadcasted_iota(jnp.int32, (CTX * NEW, 2 * Q), 1), Q)
    slot_of = lax.div(local_row, NEW)
    owner = jnp.where(
        slot_of == 0, me, jnp.where(slot_of == 1, sib, jnp.where(slot_of == 2, par, far))
    )
    fresh = owner * NEW + lax.rem(local_row, NEW) <= query
    steps(0, PAIRS, 3 * ROWS, ROWS + CTX * NEW, fresh)

    loads["wv"].wait()
    for pair in range(PAIRS):
        mean = (acc[pair] * (1.0 / total[pair])).astype(BF16)
        for side in range(2):
            head = 2 * pair + side
            out[:, head * DV : (head + 1) * DV] = lax.dot_general(
                mean[:, side * Q : (side + 1) * Q], wv[:, head * DV : (head + 1) * DV],
                (((0,), (0,)), ((), ())), preferred_element_type=F32,
            ).astype(BF16)
    for copy in to_par + to_sib + forward:
        copy.wait_send()
    store = pltpu.make_async_copy(out, o_hbm.at[0], out_sem)
    store.start()
    store.wait()


def shards(*operands):
    return pl.pallas_call(
        kernel,
        out_shape=jax.ShapeDtypeStruct((1, Q, HERE * DV), BF16),
        in_specs=[pl.BlockSpec(memory_space=pltpu.HBM)] * 9,
        out_specs=pl.BlockSpec(memory_space=pltpu.HBM),
        scratch_shapes=[
            pltpu.VMEM((Q, HERE * DH), BF16),
            pltpu.VMEM((Q, HERE * DR), BF16),
            pltpu.VMEM((DC, HERE * DH), BF16),
            pltpu.VMEM((DC, HERE * DV), BF16),
            pltpu.VMEM((NROW, DC), BF16),
            pltpu.VMEM((CTX, ROWS, DR), BF16),
            pltpu.VMEM((CTX, NEW, DR), BF16),
            pltpu.VMEM((CTX, 1, 1), jnp.int32),
            pltpu.VMEM((NROW, KEXT - DC), BF16),
            pltpu.VMEM((DC, NROW), BF16),
            pltpu.VMEM((PAIRS, KEXT, 2 * Q), BF16),
            pltpu.VMEM((PAIRS, DC, 2 * Q), F32),
            pltpu.VMEM((PAIRS, 1, 2 * Q), F32),
            pltpu.VMEM((PAIRS, 1, 2 * Q), F32),
            pltpu.VMEM((Q, HERE * DV), BF16),
            pltpu.SemaphoreType.DMA((9,)),
            pltpu.SemaphoreType.DMA,
        ]
        + [pltpu.SemaphoreType.DMA((6,))] * 6,
        compiler_params=pltpu.CompilerParams(
            collective_id=0, has_side_effects=True, vmem_limit_bytes=60 << 20
        ),
        cost_estimate=pl.CostEstimate(
            flops=7_000_000_000, bytes_accessed=7_000_000, transcendentals=2_400_000
        ),
        name="latent_attention",
    )(*operands)


def solution(mesh):
    return jax.shard_map(
        shards,
        mesh=mesh,
        in_specs=(
            P("req", None, None),
            P("req", None, None),
            P("req", "ctx", None),
            P("req", "ctx", None),
            P("req", "ctx", None),
            P("req", "ctx", None),
            P("req", "ctx"),
            P(None, "ctx"),
            P(None, "ctx"),
        ),
        out_specs=P("req", None, "ctx"),
        check_vma=False,
    )
```

```python
import functools
import math

import jax
import jax.numpy as jnp
from jax import lax
from jax.experimental import pallas as pl
from jax.experimental.pallas import tpu as pltpu
from jax.sharding import PartitionSpec as P

DC = 512
DR = 64
DH = 128
DV = 128
HEADS = 64
CTX = 4
HERE = HEADS // CTX
PAIRS = HERE // 2
Q = 128
ROWS = 256
NEW = 32
HALF = ROWS // 2
NROW = CTX * (ROWS + NEW)
KEXT = DC + 128
LOG2E = 1.4426950408889634
SCALE = LOG2E / math.sqrt(DH + DR)
BLOCKED = -1e30
MESH = pl.DeviceIdType.MESH
F32 = jnp.float32
BF16 = jnp.bfloat16

NEW0 = 2 * ROWS
FIRST = NEW0 + CTX * NEW
SECOND = FIRST + 2 * HALF
SLOT_ROWS = (
    ((0, 0, ROWS),),
    ((ROWS, 0, ROWS),),
    ((FIRST, 0, HALF), (SECOND, HALF, HALF)),
    ((FIRST + HALF, 0, HALF), (SECOND + HALF, HALF, HALF)),
)
CHUNKS = ((0, 2 * ROWS), (NEW0, CTX * NEW + 2 * HALF), (SECOND, 2 * HALF))


def kernel(
    qn_hbm, qr_hbm, cl_hbm, cr_hbm, nl_hbm, nr_hbm, len_hbm, wk_hbm, wv_hbm, o_hbm,
    qn, qr, wk, wv, lat, rope, nrope, lens, ext, latt, qt, acc, top, total, out,
    score0, score1, weight0, weight1, factor0, factor1,
    load_sem, out_sem, sib_send, sib_recv, par_send, par_recv, fwd_send, fwd_recv,
):
    me = lax.axis_index("ctx")
    sib = me + 1 - 2 * lax.rem(me, 2)
    par = lax.rem(me + 2, CTX)
    far = lax.rem(sib + 2, CTX)

    def local(index, src, dst):
        return pltpu.make_async_copy(src, dst, load_sem.at[index])

    loads = dict(
        wk=local(0, wk_hbm, wk),
        qn=local(1, qn_hbm.at[0, :, pl.ds(pl.multiple_of(me * HERE * DH, HERE * DH), HERE * DH)], qn),
        qr=local(2, qr_hbm.at[0, :, pl.ds(pl.multiple_of(me * HERE * DR, HERE * DR), HERE * DR)], qr),
        cl=local(3, cl_hbm.at[0], lat.at[pl.ds(0, ROWS)]),
        cr=local(4, cr_hbm.at[0], rope.at[0]),
        nl=local(5, nl_hbm.at[0], lat.at[pl.ds(NEW0, NEW)]),
        nr=local(6, nr_hbm.at[0], nrope.at[0]),
        ln=local(7, len_hbm, lens.at[0]),
        wv=local(8, wv_hbm, wv),
    )
    barrier = pltpu.get_barrier_semaphore()
    for peer in (sib, par):
        pl.semaphore_signal(barrier, inc=1, device_id={"ctx": peer}, device_id_type=MESH)
    for name in ("wk", "qn", "qr", "cl", "cr", "nl", "nr", "ln", "wv"):
        loads[name].start()
    pl.semaphore_wait(barrier, 2)

    def remote(src, dst, send, recv, index, peer):
        return pltpu.make_async_remote_copy(
            src_ref=src, dst_ref=dst, send_sem=send.at[index], recv_sem=recv.at[index],
            device_id={"ctx": peer}, device_id_type=MESH,
        )

    def small(slot):
        return (
            nrope.at[slot], lat.at[pl.ds(NEW0 + slot * NEW, NEW)], lens.at[slot], rope.at[slot],
        )

    mine = (nr_hbm.at[0], nl_hbm.at[0], len_hbm, cr_hbm.at[0])
    halves = tuple(cl_hbm.at[0, pl.ds(HALF * k, HALF)] for k in range(2))

    def landed(slot):
        return tuple(lat.at[pl.ds(row, count)] for row, _, count in SLOT_ROWS[slot])

    to_par = [
        remote(src, dst, par_send, par_recv, k, par)
        for k, (src, dst) in enumerate(zip(mine + halves, small(2) + landed(2)))
    ]
    to_sib = [
        remote(src, dst, sib_send, sib_recv, k, sib)
        for k, (src, dst) in enumerate(zip(mine + (cl_hbm.at[0],), small(1) + landed(1)))
    ]
    forward = [
        remote(src, dst, fwd_send, fwd_recv, k, sib)
        for k, (src, dst) in enumerate(zip(small(2) + landed(2), small(3) + landed(3)))
    ]
    for copy in to_par + to_sib:
        copy.start()

    row_of = lax.broadcasted_iota(jnp.int32, (KEXT - DC - DR, 2 * Q), 0)
    tail = jnp.where(row_of == 0, BLOCKED, 0.0).astype(BF16)
    for pair in range(PAIRS):
        qt[pair, DC + DR :, :] = tail

    loads["wk"].wait()
    loads["qn"].wait()
    loads["qr"].wait()
    for head in range(HERE):
        pair, side = head // 2, (head % 2) * Q
        part = lax.dot_general(
            wk[:, head * DH : (head + 1) * DH], qn[:, head * DH : (head + 1) * DH],
            (((1,), (1,)), ((), ())), preferred_element_type=F32,
        )
        qt[pair, :DC, side : side + Q] = part.astype(BF16)
    for pair in range(PAIRS):
        turned = qr[:, pair * 2 * DR : (pair + 1) * 2 * DR].T
        qt[pair, DC : DC + DR, :Q] = turned[:DR]
        qt[pair, DC : DC + DR, Q:] = turned[DR:]

    lane = lax.broadcasted_iota(jnp.int32, (DR, ROWS), 1)
    row = lax.broadcasted_iota(jnp.int32, (DR, ROWS), 0)

    def prepare_new(slot):
        begin = NEW0 + slot * NEW
        ext[begin : begin + NEW, :] = jnp.concatenate(
            [nrope[slot], jnp.zeros((NEW, KEXT - DC - DR), BF16)], axis=1
        )

    def prepare_cached(slot):
        live = jnp.broadcast_to(lens[slot], (DR, ROWS))
        dead = jnp.where((row == 0) & (lane >= live), 1.0, 0.0).astype(BF16)
        wide = jnp.concatenate([rope[slot], dead], axis=0).T
        for begin, first, count in SLOT_ROWS[slot]:
            ext[begin : begin + count, :] = wide[first : first + count]

    def turn(begin, count):
        latt[:, begin : begin + count] = lat[begin : begin + count, :].T

    local_row = lax.broadcasted_iota(jnp.int32, (CTX * NEW, 2 * Q), 0)
    query = lax.rem(lax.broadcasted_iota(jnp.int32, (CTX * NEW, 2 * Q), 1), Q)
    slot_of = lax.div(local_row, NEW)
    owner = jnp.where(
        slot_of == 0, me, jnp.where(slot_of == 1, sib, jnp.where(slot_of == 2, par, far))
    )
    fresh = owner * NEW + lax.rem(local_row, NEW) <= query

    score, weight, factor = (score0, score1), (weight0, weight1), (factor0, factor1)
    items = [(chunk, pair) for chunk in range(len(CHUNKS)) for pair in range(PAIRS)]

    def score_of(index):
        chunk, pair = items[index]
        begin, count = CHUNKS[chunk]
        keys = jnp.concatenate(
            [lat[begin : begin + count, :], ext[begin : begin + count, :]], axis=1
        )
        score[index % 2][:count] = jnp.dot(keys, qt[pair], preferred_element_type=F32)

    def weigh(index):
        chunk, pair = items[index]
        begin, count = CHUNKS[chunk]
        scores = score[index % 2][:count]
        if begin == NEW0:
            new = CTX * NEW
            scores = jnp.concatenate([jnp.where(fresh, scores[:new], BLOCKED), scores[new:]], axis=0)
        level = jnp.max(scores, axis=0, keepdims=True)
        if chunk:
            level = jnp.maximum(top[pair], level)
            change = jnp.exp2((top[pair] - level) * SCALE)
            factor[index % 2][...] = change
        weights = jnp.exp2((scores - level) * SCALE)
        sums = jnp.sum(weights, axis=0, keepdims=True)
        top[pair] = level
        total[pair] = total[pair] * change + sums if chunk else sums
        weight[index % 2][:count] = weights.astype(BF16)

    def gather_in(index):
        chunk, pair = items[index]
        begin, count = CHUNKS[chunk]
        part = jnp.dot(
            latt[:, begin : begin + count], weight[index % 2][:count], preferred_element_type=F32
        )
        acc[pair] = acc[pair] * factor[index % 2][...] + part if chunk else part

    def onward(indices):
        for k in indices:
            to_par[k].wait_recv()
            forward[k].start()

    def before_item(index):
        if index == 0:
            for name in ("cl", "cr", "nl", "nr", "ln"):
                loads[name].wait()
            for copy in to_sib:
                copy.wait_recv()
            for slot in range(2):
                prepare_new(slot)
                prepare_cached(slot)
            turn(0, NEW0)
        if index == 3:
            onward(range(4))
        if index == PAIRS:
            onward(range(4, 5))
            for copy in forward[:5]:
                copy.wait_recv()
            for slot in range(2, 4):
                prepare_new(slot)
                prepare_cached(slot)
            turn(NEW0, SECOND - NEW0)
        if index == 2 * PAIRS - 3:
            onward(range(5, 6))
        if index == 2 * PAIRS:
            forward[5].wait_recv()
            turn(SECOND, NROW - SECOND)

    for index in range(len(items) + 2):
        if index < len(items):
            before_item(index)
            score_of(index)
        if 1 <= index <= len(items):
            weigh(index - 1)
        if index >= 2:
            gather_in(index - 2)

    loads["wv"].wait()
    for pair in range(PAIRS):
        mean = (acc[pair] * (1.0 / total[pair])).astype(BF16)
        for side in range(2):
            head = 2 * pair + side
            out[:, head * DV : (head + 1) * DV] = lax.dot_general(
                mean[:, side * Q : (side + 1) * Q], wv[:, head * DV : (head + 1) * DV],
                (((0,), (0,)), ((), ())), preferred_element_type=F32,
            ).astype(BF16)
    for copy in to_par + to_sib + forward:
        copy.wait_send()
    store = pltpu.make_async_copy(out, o_hbm.at[0], out_sem)
    store.start()
    store.wait()


def shards(*operands):
    operands = operands[:3] + (jnp.swapaxes(operands[3], 1, 2),) + operands[4:]
    return pl.pallas_call(
        kernel,
        out_shape=jax.ShapeDtypeStruct((1, Q, HERE * DV), BF16),
        in_specs=[pl.BlockSpec(memory_space=pltpu.HBM)] * 9,
        out_specs=pl.BlockSpec(memory_space=pltpu.HBM),
        scratch_shapes=[
            pltpu.VMEM((Q, HERE * DH), BF16),
            pltpu.VMEM((Q, HERE * DR), BF16),
            pltpu.VMEM((DC, HERE * DH), BF16),
            pltpu.VMEM((DC, HERE * DV), BF16),
            pltpu.VMEM((NROW, DC), BF16),
            pltpu.VMEM((CTX, DR, ROWS), BF16),
            pltpu.VMEM((CTX, NEW, DR), BF16),
            pltpu.VMEM((CTX, 1, 1), jnp.int32),
            pltpu.VMEM((NROW, KEXT - DC), BF16),
            pltpu.VMEM((DC, NROW), BF16),
            pltpu.VMEM((PAIRS, KEXT, 2 * Q), BF16),
            pltpu.VMEM((PAIRS, DC, 2 * Q), F32),
            pltpu.VMEM((PAIRS, 1, 2 * Q), F32),
            pltpu.VMEM((PAIRS, 1, 2 * Q), F32),
            pltpu.VMEM((Q, HERE * DV), BF16),
            pltpu.VMEM((2 * ROWS, 2 * Q), F32),
            pltpu.VMEM((2 * ROWS, 2 * Q), F32),
            pltpu.VMEM((2 * ROWS, 2 * Q), BF16),
            pltpu.VMEM((2 * ROWS, 2 * Q), BF16),
            pltpu.VMEM((1, 2 * Q), F32),
            pltpu.VMEM((1, 2 * Q), F32),
            pltpu.SemaphoreType.DMA((9,)),
            pltpu.SemaphoreType.DMA,
        ]
        + [pltpu.SemaphoreType.DMA((6,))] * 6,
        compiler_params=pltpu.CompilerParams(
            collective_id=0, has_side_effects=True, vmem_limit_bytes=60 << 20
        ),
        cost_estimate=pl.CostEstimate(
            flops=7_000_000_000, bytes_accessed=7_000_000, transcendentals=2_400_000
        ),
        name="latent_attention",
    )(*operands)


def solution(mesh):
    return jax.shard_map(
        shards,
        mesh=mesh,
        in_specs=(
            P("req", None, None),
            P("req", None, None),
            P("req", "ctx", None),
            P("req", "ctx", None),
            P("req", "ctx", None),
            P("req", "ctx", None),
            P("req", "ctx"),
            P(None, "ctx"),
            P(None, "ctx"),
        ),
        out_specs=P("req", None, "ctx"),
        check_vma=False,
    )
```

```python
import functools
import math

import jax
import jax.numpy as jnp
from jax import lax
from jax.experimental import pallas as pl
from jax.experimental.pallas import tpu as pltpu
from jax.sharding import PartitionSpec as P

DC = 512
DR = 64
DH = 128
DV = 128
HEADS = 64
CTX = 4
HERE = HEADS // CTX
PAIRS = HERE // 2
Q = 128
ROWS = 256
NEW = 32
HALF = ROWS // 2
NROW = CTX * (ROWS + NEW)
KEXT = DC + 128
LOG2E = 1.4426950408889634
SCALE = LOG2E / math.sqrt(DH + DR)
BLOCKED = -1e30
MESH = pl.DeviceIdType.MESH
F32 = jnp.float32
BF16 = jnp.bfloat16

NEW0 = 2 * ROWS
FIRST = NEW0 + CTX * NEW
SECOND = FIRST + 2 * HALF
SLOT_ROWS = (
    ((0, 0, ROWS),),
    ((ROWS, 0, ROWS),),
    ((FIRST, 0, HALF), (SECOND, HALF, HALF)),
    ((FIRST + HALF, 0, HALF), (SECOND + HALF, HALF, HALF)),
)
CHUNKS = ((0, 2 * ROWS), (NEW0, CTX * NEW + 2 * HALF), (SECOND, 2 * HALF))


def kernel(
    qn_hbm, qr_hbm, cl_hbm, cr_hbm, nl_hbm, nr_hbm, len_hbm, wk_hbm, wv_hbm, out,
    qn, qr, wk, wv, lat, rope, nrope, lens, ext, latt, qt, acc, top, total,
    score0, score1, weight0, weight1, factor0, factor1,
    load_sem, sib_send, sib_recv, par_send, par_recv, fwd_send, fwd_recv,
):
    me = lax.axis_index("ctx")
    sib = me + 1 - 2 * lax.rem(me, 2)
    par = lax.rem(me + 2, CTX)
    far = lax.rem(sib + 2, CTX)

    def local(index, src, dst):
        return pltpu.make_async_copy(src, dst, load_sem.at[index])

    loads = dict(
        wk=local(0, wk_hbm, wk),
        qn=local(1, qn_hbm.at[0, :, pl.ds(pl.multiple_of(me * HERE * DH, HERE * DH), HERE * DH)], qn),
        qr=local(2, qr_hbm.at[0, :, pl.ds(pl.multiple_of(me * HERE * DR, HERE * DR), HERE * DR)], qr),
        cl=local(3, cl_hbm.at[0], lat.at[pl.ds(0, ROWS)]),
        cr=local(4, cr_hbm.at[0], rope.at[0]),
        nl=local(5, nl_hbm.at[0], lat.at[pl.ds(NEW0, NEW)]),
        nr=local(6, nr_hbm.at[0], nrope.at[0]),
        ln=local(7, len_hbm, lens.at[0]),
        wv=local(8, wv_hbm, wv),
    )
    barrier = pltpu.get_barrier_semaphore()
    for peer in (sib, par):
        pl.semaphore_signal(barrier, inc=1, device_id={"ctx": peer}, device_id_type=MESH)
    for name in ("wk", "qn", "qr", "cl", "cr", "nl", "nr", "ln", "wv"):
        loads[name].start()
    pl.semaphore_wait(barrier, 2)

    def remote(src, dst, send, recv, index, peer):
        return pltpu.make_async_remote_copy(
            src_ref=src, dst_ref=dst, send_sem=send.at[index], recv_sem=recv.at[index],
            device_id={"ctx": peer}, device_id_type=MESH,
        )

    def small(slot):
        return (
            nrope.at[slot], lat.at[pl.ds(NEW0 + slot * NEW, NEW)], lens.at[slot], rope.at[slot],
        )

    mine = (nr_hbm.at[0], nl_hbm.at[0], len_hbm, cr_hbm.at[0])
    halves = tuple(cl_hbm.at[0, pl.ds(HALF * k, HALF)] for k in range(2))

    def landed(slot):
        return tuple(lat.at[pl.ds(row, count)] for row, _, count in SLOT_ROWS[slot])

    to_par = [
        remote(src, dst, par_send, par_recv, k, par)
        for k, (src, dst) in enumerate(zip(mine + halves, small(2) + landed(2)))
    ]
    to_sib = [
        remote(src, dst, sib_send, sib_recv, k, sib)
        for k, (src, dst) in enumerate(zip(mine + (cl_hbm.at[0],), small(1) + landed(1)))
    ]
    forward = [
        remote(src, dst, fwd_send, fwd_recv, k, sib)
        for k, (src, dst) in enumerate(zip(small(2) + landed(2), small(3) + landed(3)))
    ]
    for copy in to_par + to_sib:
        copy.start()

    row_of = lax.broadcasted_iota(jnp.int32, (KEXT - DC - DR, 2 * Q), 0)
    tail = jnp.where(row_of == 0, BLOCKED, 0.0).astype(BF16)
    for pair in range(PAIRS):
        qt[pair, DC + DR :, :] = tail

    loads["wk"].wait()
    loads["qn"].wait()
    loads["qr"].wait()
    for head in range(HERE):
        pair, side = head // 2, (head % 2) * Q
        part = lax.dot_general(
            wk[:, head * DH : (head + 1) * DH], qn[:, head * DH : (head + 1) * DH],
            (((1,), (1,)), ((), ())), preferred_element_type=F32,
        )
        qt[pair, :DC, side : side + Q] = part.astype(BF16)
    for pair in range(PAIRS):
        turned = qr[:, pair * 2 * DR : (pair + 1) * 2 * DR].T
        qt[pair, DC : DC + DR, :Q] = turned[:DR]
        qt[pair, DC : DC + DR, Q:] = turned[DR:]

    lane = lax.broadcasted_iota(jnp.int32, (DR, ROWS), 1)
    row = lax.broadcasted_iota(jnp.int32, (DR, ROWS), 0)

    def prepare_new(slot):
        begin = NEW0 + slot * NEW
        ext[begin : begin + NEW, :] = jnp.concatenate(
            [nrope[slot], jnp.zeros((NEW, KEXT - DC - DR), BF16)], axis=1
        )

    def prepare_cached(slot):
        live = jnp.broadcast_to(lens[slot], (DR, ROWS))
        dead = jnp.where((row == 0) & (lane >= live), 1.0, 0.0).astype(BF16)
        wide = jnp.concatenate([rope[slot], dead], axis=0).T
        for begin, first, count in SLOT_ROWS[slot]:
            ext[begin : begin + count, :] = wide[first : first + count]

    def turn(begin, count):
        latt[:, begin : begin + count] = lat[begin : begin + count, :].T

    local_row = lax.broadcasted_iota(jnp.int32, (CTX * NEW, 2 * Q), 0)
    query = lax.rem(lax.broadcasted_iota(jnp.int32, (CTX * NEW, 2 * Q), 1), Q)
    slot_of = lax.div(local_row, NEW)
    owner = jnp.where(
        slot_of == 0, me, jnp.where(slot_of == 1, sib, jnp.where(slot_of == 2, par, far))
    )
    fresh = owner * NEW + lax.rem(local_row, NEW) <= query

    score, weight, factor = (score0, score1), (weight0, weight1), (factor0, factor1)
    items = [(chunk, pair) for chunk in range(len(CHUNKS)) for pair in range(PAIRS)]

    def score_of(index):
        chunk, pair = items[index]
        begin, count = CHUNKS[chunk]
        keys = jnp.concatenate(
            [lat[begin : begin + count, :], ext[begin : begin + count, :]], axis=1
        )
        score[index % 2][:count] = jnp.dot(keys, qt[pair], preferred_element_type=F32)

    def weigh(index):
        chunk, pair = items[index]
        begin, count = CHUNKS[chunk]
        scores = score[index % 2][:count]
        if begin == NEW0:
            new = CTX * NEW
            scores = jnp.concatenate([jnp.where(fresh, scores[:new], BLOCKED), scores[new:]], axis=0)
        level = jnp.max(scores, axis=0, keepdims=True)
        if chunk:
            level = jnp.maximum(top[pair], level)
            change = jnp.exp2((top[pair] - level) * SCALE)
            factor[index % 2][...] = change
        weights = jnp.exp2((scores - level) * SCALE)
        sums = jnp.sum(weights, axis=0, keepdims=True)
        top[pair] = level
        total[pair] = total[pair] * change + sums if chunk else sums
        weight[index % 2][:count] = weights.astype(BF16)

    def gather_in(index):
        chunk, pair = items[index]
        begin, count = CHUNKS[chunk]
        part = jnp.dot(
            latt[:, begin : begin + count], weight[index % 2][:count], preferred_element_type=F32
        )
        acc[pair] = acc[pair] * factor[index % 2][...] + part if chunk else part

    def onward(indices):
        for k in indices:
            to_par[k].wait_recv()
            forward[k].start()

    def before_item(index):
        if index == 0:
            for name in ("cl", "cr", "nl", "nr", "ln"):
                loads[name].wait()
            for copy in to_sib:
                copy.wait_recv()
            for slot in range(2):
                prepare_new(slot)
                prepare_cached(slot)
            turn(0, NEW0)
        if index == 3:
            onward(range(4))
        if index == PAIRS:
            onward(range(4, 5))
            for copy in forward[:5]:
                copy.wait_recv()
            for slot in range(2, 4):
                prepare_new(slot)
                prepare_cached(slot)
            turn(NEW0, SECOND - NEW0)
        if index == 2 * PAIRS - 3:
            onward(range(5, 6))
        if index == 2 * PAIRS:
            forward[5].wait_recv()
            turn(SECOND, NROW - SECOND)

    for index in range(len(items) + 2):
        if index < len(items):
            before_item(index)
            score_of(index)
        if 1 <= index <= len(items):
            weigh(index - 1)
        if index >= 2:
            gather_in(index - 2)

    loads["wv"].wait()
    for pair in range(PAIRS):
        mean = (acc[pair] * (1.0 / total[pair])).astype(BF16)
        for side in range(2):
            head = 2 * pair + side
            out[0, :, head * DV : (head + 1) * DV] = lax.dot_general(
                mean[:, side * Q : (side + 1) * Q], wv[:, head * DV : (head + 1) * DV],
                (((0,), (0,)), ((), ())), preferred_element_type=F32,
            ).astype(BF16)
    for copy in to_par + to_sib + forward:
        copy.wait_send()


def shards(*operands):
    operands = operands[:3] + (jnp.swapaxes(operands[3], 1, 2),) + operands[4:]
    operands = tuple(
        x if index == 6 else pltpu.with_memory_space_constraint(x, pltpu.HBM)
        for index, x in enumerate(operands)
    )
    return pl.pallas_call(
        kernel,
        out_shape=pltpu.VMEM((1, Q, HERE * DV), BF16),
        in_specs=[pl.BlockSpec(memory_space=pltpu.HBM)] * 9,
        out_specs=pl.BlockSpec(memory_space=pltpu.VMEM),
        scratch_shapes=[
            pltpu.VMEM((Q, HERE * DH), BF16),
            pltpu.VMEM((Q, HERE * DR), BF16),
            pltpu.VMEM((DC, HERE * DH), BF16),
            pltpu.VMEM((DC, HERE * DV), BF16),
            pltpu.VMEM((NROW, DC), BF16),
            pltpu.VMEM((CTX, DR, ROWS), BF16),
            pltpu.VMEM((CTX, NEW, DR), BF16),
            pltpu.VMEM((CTX, 1, 1), jnp.int32),
            pltpu.VMEM((NROW, KEXT - DC), BF16),
            pltpu.VMEM((DC, NROW), BF16),
            pltpu.VMEM((PAIRS, KEXT, 2 * Q), BF16),
            pltpu.VMEM((PAIRS, DC, 2 * Q), F32),
            pltpu.VMEM((PAIRS, 1, 2 * Q), F32),
            pltpu.VMEM((PAIRS, 1, 2 * Q), F32),
            pltpu.VMEM((2 * ROWS, 2 * Q), F32),
            pltpu.VMEM((2 * ROWS, 2 * Q), F32),
            pltpu.VMEM((2 * ROWS, 2 * Q), BF16),
            pltpu.VMEM((2 * ROWS, 2 * Q), BF16),
            pltpu.VMEM((1, 2 * Q), F32),
            pltpu.VMEM((1, 2 * Q), F32),
            pltpu.SemaphoreType.DMA((9,)),
        ]
        + [pltpu.SemaphoreType.DMA((6,))] * 6,
        compiler_params=pltpu.CompilerParams(
            collective_id=0, has_side_effects=True, vmem_limit_bytes=40 << 20
        ),
        cost_estimate=pl.CostEstimate(
            flops=7_000_000_000, bytes_accessed=7_000_000, transcendentals=2_400_000
        ),
        name="latent_attention",
    )(*operands)


def solution(mesh):
    return jax.shard_map(
        shards,
        mesh=mesh,
        in_specs=(
            P("req", None, None),
            P("req", None, None),
            P("req", "ctx", None),
            P("req", "ctx", None),
            P("req", "ctx", None),
            P("req", "ctx", None),
            P("req", "ctx"),
            P(None, "ctx"),
            P(None, "ctx"),
        ),
        out_specs=P("req", None, "ctx"),
        check_vma=False,
    )
```

```python
import functools
import math

import jax
import jax.numpy as jnp
from jax import lax
from jax.experimental import pallas as pl
from jax.experimental.pallas import tpu as pltpu
from jax.sharding import PartitionSpec as P

DC = 512
DR = 64
DH = 128
DV = 128
HEADS = 64
CTX = 4
HERE = HEADS // CTX
PAIRS = HERE // 2
Q = 128
ROWS = 256
NEW = 32
HALF = ROWS // 2
NROW = CTX * (ROWS + NEW)
KEXT = DC + 128
LOG2E = 1.4426950408889634
SCALE = LOG2E / math.sqrt(DH + DR)
BLOCKED = -1e30
MESH = pl.DeviceIdType.MESH
F32 = jnp.float32
BF16 = jnp.bfloat16

NEW0 = 2 * ROWS
FAR0 = NEW0 + CTX * NEW
SLOT_ROWS = (
    ((0, 0, ROWS),),
    ((ROWS, 0, ROWS),),
    ((FAR0, 0, HALF), (FAR0 + 2 * HALF, HALF, HALF)),
    ((FAR0 + HALF, 0, HALF), (FAR0 + 3 * HALF, HALF, HALF)),
)
CHUNKS = (
    (0, 2 * ROWS),
    (NEW0, CTX * NEW + HALF),
    (FAR0 + HALF, 2 * HALF),
    (FAR0 + 3 * HALF, HALF),
)


def kernel(
    qn_hbm, qr_hbm, cl_hbm, cr_hbm, nl_hbm, nr_hbm, len_hbm, wk_hbm, wv_hbm, out,
    qn, qr, wk, wv, lat, rope, nrope, lens, ext, latt, qt, acc, top, total,
    score0, score1, weight0, weight1, factor0, factor1,
    load_sem, sib_send, sib_recv, par_send, par_recv, fwd_send, fwd_recv,
):
    me = lax.axis_index("ctx")
    sib = me + 1 - 2 * lax.rem(me, 2)
    par = lax.rem(me + 2, CTX)
    far = lax.rem(sib + 2, CTX)

    def local(index, src, dst):
        return pltpu.make_async_copy(src, dst, load_sem.at[index])

    loads = dict(
        wk=local(0, wk_hbm, wk),
        qn=local(1, qn_hbm.at[0, :, pl.ds(pl.multiple_of(me * HERE * DH, HERE * DH), HERE * DH)], qn),
        qr=local(2, qr_hbm.at[0, :, pl.ds(pl.multiple_of(me * HERE * DR, HERE * DR), HERE * DR)], qr),
        cl=local(3, cl_hbm.at[0], lat.at[pl.ds(0, ROWS)]),
        cr=local(4, cr_hbm.at[0], rope.at[0]),
        nl=local(5, nl_hbm.at[0], lat.at[pl.ds(NEW0, NEW)]),
        nr=local(6, nr_hbm.at[0], nrope.at[0]),
        ln=local(7, len_hbm, lens.at[0]),
        wv=local(8, wv_hbm, wv),
    )
    barrier = pltpu.get_barrier_semaphore()
    for peer in (sib, par):
        pl.semaphore_signal(barrier, inc=1, device_id={"ctx": peer}, device_id_type=MESH)
    for name in ("wk", "qn", "qr", "cl", "cr", "nl", "nr", "ln"):
        loads[name].start()
    pl.semaphore_wait(barrier, 2)

    def remote(src, dst, send, recv, index, peer):
        return pltpu.make_async_remote_copy(
            src_ref=src, dst_ref=dst, send_sem=send.at[index], recv_sem=recv.at[index],
            device_id={"ctx": peer}, device_id_type=MESH,
        )

    def small(slot):
        return (
            nrope.at[slot], lat.at[pl.ds(NEW0 + slot * NEW, NEW)], lens.at[slot], rope.at[slot],
        )

    mine = (nr_hbm.at[0], nl_hbm.at[0], len_hbm, cr_hbm.at[0])
    halves = tuple(cl_hbm.at[0, pl.ds(HALF * k, HALF)] for k in range(2))

    def landed(slot):
        return tuple(lat.at[pl.ds(row, count)] for row, _, count in SLOT_ROWS[slot])

    to_par = [
        remote(src, dst, par_send, par_recv, k, par)
        for k, (src, dst) in enumerate(zip(mine + halves, small(2) + landed(2)))
    ]
    to_sib = [
        remote(src, dst, sib_send, sib_recv, k, sib)
        for k, (src, dst) in enumerate(zip(mine + (cl_hbm.at[0],), small(1) + landed(1)))
    ]
    forward = [
        remote(src, dst, fwd_send, fwd_recv, k, sib)
        for k, (src, dst) in enumerate(zip(small(2) + landed(2), small(3) + landed(3)))
    ]
    for copy in to_par + to_sib:
        copy.start()
    loads["wv"].start()

    row_of = lax.broadcasted_iota(jnp.int32, (KEXT - DC - DR, 2 * Q), 0)
    tail = jnp.where(row_of == 0, BLOCKED, 0.0).astype(BF16)
    for pair in range(PAIRS):
        qt[pair, DC + DR :, :] = tail

    loads["wk"].wait()
    loads["qn"].wait()
    loads["qr"].wait()
    for head in range(HERE):
        pair, side = head // 2, (head % 2) * Q
        part = lax.dot_general(
            wk[:, head * DH : (head + 1) * DH], qn[:, head * DH : (head + 1) * DH],
            (((1,), (1,)), ((), ())), preferred_element_type=F32,
        )
        qt[pair, :DC, side : side + Q] = part.astype(BF16)
    for pair in range(PAIRS):
        turned = qr[:, pair * 2 * DR : (pair + 1) * 2 * DR].T
        qt[pair, DC : DC + DR, :Q] = turned[:DR]
        qt[pair, DC : DC + DR, Q:] = turned[DR:]

    lane = lax.broadcasted_iota(jnp.int32, (DR, ROWS), 1)
    row = lax.broadcasted_iota(jnp.int32, (DR, ROWS), 0)

    def prepare_new(slot):
        begin = NEW0 + slot * NEW
        ext[begin : begin + NEW, :] = jnp.concatenate(
            [nrope[slot], jnp.zeros((NEW, KEXT - DC - DR), BF16)], axis=1
        )

    def prepare_cached(slot):
        live = jnp.broadcast_to(lens[slot], (DR, ROWS))
        dead = jnp.where((row == 0) & (lane >= live), 1.0, 0.0).astype(BF16)
        wide = jnp.concatenate([rope[slot], dead], axis=0).T
        for begin, first, count in SLOT_ROWS[slot]:
            ext[begin : begin + count, :] = wide[first : first + count]

    def turn(begin, count):
        latt[:, begin : begin + count] = lat[begin : begin + count, :].T

    local_row = lax.broadcasted_iota(jnp.int32, (CTX * NEW, 2 * Q), 0)
    query = lax.rem(lax.broadcasted_iota(jnp.int32, (CTX * NEW, 2 * Q), 1), Q)
    slot_of = lax.div(local_row, NEW)
    owner = jnp.where(
        slot_of == 0, me, jnp.where(slot_of == 1, sib, jnp.where(slot_of == 2, par, far))
    )
    fresh = owner * NEW + lax.rem(local_row, NEW) <= query

    score, weight, factor = (score0, score1), (weight0, weight1), (factor0, factor1)
    items = [(chunk, pair) for chunk in range(len(CHUNKS)) for pair in range(PAIRS)]

    def score_of(index):
        chunk, pair = items[index]
        begin, count = CHUNKS[chunk]
        keys = jnp.concatenate(
            [lat[begin : begin + count, :], ext[begin : begin + count, :]], axis=1
        )
        score[index % 2][:count] = jnp.dot(keys, qt[pair], preferred_element_type=F32)

    def weigh(index):
        chunk, pair = items[index]
        begin, count = CHUNKS[chunk]
        scores = score[index % 2][:count]
        if begin == NEW0:
            new = CTX * NEW
            scores = jnp.concatenate([jnp.where(fresh, scores[:new], BLOCKED), scores[new:]], axis=0)
        level = jnp.max(scores, axis=0, keepdims=True)
        if chunk:
            level = jnp.maximum(top[pair], level)
            change = jnp.exp2((top[pair] - level) * SCALE)
            factor[index % 2][...] = change
        weights = jnp.exp2((scores - level) * SCALE)
        sums = jnp.sum(weights, axis=0, keepdims=True)
        top[pair] = level
        total[pair] = total[pair] * change + sums if chunk else sums
        weight[index % 2][:count] = weights.astype(BF16)

    def gather_in(index):
        chunk, pair = items[index]
        begin, count = CHUNKS[chunk]
        part = jnp.dot(
            latt[:, begin : begin + count], weight[index % 2][:count], preferred_element_type=F32
        )
        acc[pair] = acc[pair] * factor[index % 2][...] + part if chunk else part

    def finish(index):
        pair = items[index][1]
        mean = (acc[pair] * (1.0 / total[pair])).astype(BF16)
        for side in range(2):
            head = 2 * pair + side
            out[0, :, head * DV : (head + 1) * DV] = lax.dot_general(
                mean[:, side * Q : (side + 1) * Q], wv[:, head * DV : (head + 1) * DV],
                (((0,), (0,)), ((), ())), preferred_element_type=F32,
            ).astype(BF16)

    def onward(indices):
        for k in indices:
            to_par[k].wait_recv()
            forward[k].start()

    def before_item(index):
        if index == 0:
            for name in ("cl", "cr", "nl", "nr", "ln"):
                loads[name].wait()
            for copy in to_sib:
                copy.wait_recv()
            for slot in range(2):
                prepare_new(slot)
                prepare_cached(slot)
            turn(*CHUNKS[0])
        if index == 5:
            onward(range(4))
        if index == PAIRS:
            onward(range(4, 5))
            for copy in forward[:4]:
                copy.wait_recv()
            for slot in range(2, 4):
                prepare_new(slot)
                prepare_cached(slot)
            turn(*CHUNKS[1])
        if index == 2 * PAIRS:
            onward(range(5, 6))
            forward[4].wait_recv()
            turn(*CHUNKS[2])
        if index == 3 * PAIRS:
            forward[5].wait_recv()
            loads["wv"].wait()
            turn(*CHUNKS[3])

    stages = (score_of, weigh, gather_in)
    done = [0, 0, 0]

    def advance(stage, index):
        if done[stage] <= index < len(items):
            assert done[stage] == index
            done[stage] += 1
            stages[stage](index)

    last = len(items) - PAIRS
    for index in range(len(items) + 3):
        if index in (PAIRS, 2 * PAIRS):
            advance(1, index - 1)
            advance(2, index - 2)
            advance(2, index - 1)
        before_item(index)
        advance(0, index)
        if index >= 1:
            advance(1, index - 1)
        if index >= 2:
            advance(2, index - 2)
        if index >= last + 3:
            finish(index - 3)
    for copy in to_par + to_sib + forward:
        copy.wait_send()


def shards(*operands):
    operands = operands[:3] + (jnp.swapaxes(operands[3], 1, 2),) + operands[4:]
    operands = tuple(
        x if index == 6 else pltpu.with_memory_space_constraint(x, pltpu.HBM)
        for index, x in enumerate(operands)
    )
    return pl.pallas_call(
        kernel,
        out_shape=pltpu.VMEM((1, Q, HERE * DV), BF16),
        in_specs=[pl.BlockSpec(memory_space=pltpu.HBM)] * 9,
        out_specs=pl.BlockSpec(memory_space=pltpu.VMEM),
        scratch_shapes=[
            pltpu.VMEM((Q, HERE * DH), BF16),
            pltpu.VMEM((Q, HERE * DR), BF16),
            pltpu.VMEM((DC, HERE * DH), BF16),
            pltpu.VMEM((DC, HERE * DV), BF16),
            pltpu.VMEM((NROW, DC), BF16),
            pltpu.VMEM((CTX, DR, ROWS), BF16),
            pltpu.VMEM((CTX, NEW, DR), BF16),
            pltpu.VMEM((CTX, 1, 1), jnp.int32),
            pltpu.VMEM((NROW, KEXT - DC), BF16),
            pltpu.VMEM((DC, NROW), BF16),
            pltpu.VMEM((PAIRS, KEXT, 2 * Q), BF16),
            pltpu.VMEM((PAIRS, DC, 2 * Q), F32),
            pltpu.VMEM((PAIRS, 1, 2 * Q), F32),
            pltpu.VMEM((PAIRS, 1, 2 * Q), F32),
            pltpu.VMEM((2 * ROWS, 2 * Q), F32),
            pltpu.VMEM((2 * ROWS, 2 * Q), F32),
            pltpu.VMEM((2 * ROWS, 2 * Q), BF16),
            pltpu.VMEM((2 * ROWS, 2 * Q), BF16),
            pltpu.VMEM((1, 2 * Q), F32),
            pltpu.VMEM((1, 2 * Q), F32),
            pltpu.SemaphoreType.DMA((9,)),
        ]
        + [pltpu.SemaphoreType.DMA((6,))] * 6,
        compiler_params=pltpu.CompilerParams(
            collective_id=0, has_side_effects=True, vmem_limit_bytes=40 << 20
        ),
        cost_estimate=pl.CostEstimate(
            flops=7_000_000_000, bytes_accessed=7_000_000, transcendentals=2_400_000
        ),
        name="latent_attention",
    )(*operands)


def solution(mesh):
    return jax.shard_map(
        shards,
        mesh=mesh,
        in_specs=(
            P("req", None, None),
            P("req", None, None),
            P("req", "ctx", None),
            P("req", "ctx", None),
            P("req", "ctx", None),
            P("req", "ctx", None),
            P("req", "ctx"),
            P(None, "ctx"),
            P(None, "ctx"),
        ),
        out_specs=P("req", None, "ctx"),
        check_vma=False,
    )
```

```python
import functools
import math

import jax
import jax.numpy as jnp
from jax import lax
from jax.experimental import pallas as pl
from jax.experimental.pallas import tpu as pltpu
from jax.sharding import PartitionSpec as P

DC = 512
DR = 64
DH = 128
DV = 128
HEADS = 64
CTX = 4
HERE = HEADS // CTX
PAIRS = HERE // 2
Q = 128
ROWS = 256
NEW = 32
NROW = CTX * (ROWS + NEW)
KEXT = DC + 128
LOG2E = 1.4426950408889634
SCALE = LOG2E / math.sqrt(DH + DR)
BLOCKED = -1e30
MESH = pl.DeviceIdType.MESH
F32 = jnp.float32
BF16 = jnp.bfloat16

PIECES = (128, 80, 48)
STARTS = (0, 128, 208)
RELAYED = 2
NEW0 = 2 * ROWS
FAR0 = NEW0 + CTX * NEW
LANDS = (
    None,
    (ROWS,),
    (FAR0, FAR0 + 2 * PIECES[0], FAR0 + 2 * PIECES[0] + 2 * PIECES[1]),
    (FAR0 + PIECES[0], FAR0 + 2 * PIECES[0] + PIECES[1], FAR0 + 2 * PIECES[0] + 2 * PIECES[1] + PIECES[2]),
)
SLOT_ROWS = (
    ((0, 0, ROWS),),
    ((ROWS, 0, ROWS),),
    tuple(zip(LANDS[2], STARTS, PIECES)),
    tuple(zip(LANDS[3], STARTS, PIECES)),
)
CHUNKS = (
    (0, 2 * ROWS, 0, 2 * ROWS),
    (NEW0, CTX * NEW + PIECES[0], 512, 256),
    (LANDS[3][0], PIECES[0] + PIECES[1], 768, 256),
    (LANDS[3][1], PIECES[1] + 2 * PIECES[2], 1024, 256),
)
TURNED = 1280


def kernel(
    qn_hbm, qr_hbm, cl_hbm, cr_hbm, nl_hbm, nr_hbm, len_hbm, wk_hbm, wv_hbm, out,
    qn, qr, wk, wv, lat, rope, nrope, lens, ext, latt, qt, acc, top, total,
    score0, score1, weight0, weight1, factor0, factor1,
    load_sem, sib_send, sib_recv, par_send, par_recv, fwd_send, fwd_recv, far_send, far_recv,
):
    me = lax.axis_index("ctx")
    sib = me + 1 - 2 * lax.rem(me, 2)
    par = lax.rem(me + 2, CTX)
    far = lax.rem(sib + 2, CTX)

    def local(index, src, dst):
        return pltpu.make_async_copy(src, dst, load_sem.at[index])

    loads = dict(
        wk=local(0, wk_hbm, wk),
        qn=local(1, qn_hbm.at[0, :, pl.ds(pl.multiple_of(me * HERE * DH, HERE * DH), HERE * DH)], qn),
        qr=local(2, qr_hbm.at[0, :, pl.ds(pl.multiple_of(me * HERE * DR, HERE * DR), HERE * DR)], qr),
        cl=local(3, cl_hbm.at[0], lat.at[pl.ds(0, ROWS)]),
        cr=local(4, cr_hbm.at[0], rope.at[0]),
        nl=local(5, nl_hbm.at[0], lat.at[pl.ds(NEW0, NEW)]),
        nr=local(6, nr_hbm.at[0], nrope.at[0]),
        ln=local(7, len_hbm, lens.at[0]),
        wv=local(8, wv_hbm, wv),
    )
    barrier = pltpu.get_barrier_semaphore()
    for peer in (sib, par, far):
        pl.semaphore_signal(barrier, inc=1, device_id={"ctx": peer}, device_id_type=MESH)
    for name in ("wk", "qn", "qr", "cl", "cr", "nl", "nr", "ln"):
        loads[name].start()
    pl.semaphore_wait(barrier, 3)

    def remote(src, dst, send, recv, index, peer):
        return pltpu.make_async_remote_copy(
            src_ref=src, dst_ref=dst, send_sem=send.at[index], recv_sem=recv.at[index],
            device_id={"ctx": peer}, device_id_type=MESH,
        )

    def small(slot):
        return (
            nrope.at[slot], lat.at[pl.ds(NEW0 + slot * NEW, NEW)], lens.at[slot], rope.at[slot],
        )

    mine = (nr_hbm.at[0], nl_hbm.at[0], len_hbm, cr_hbm.at[0])
    pieces = tuple(cl_hbm.at[0, pl.ds(start, count)] for start, count in zip(STARTS, PIECES))

    def landed(slot):
        return tuple(lat.at[pl.ds(row, count)] for row, _, count in SLOT_ROWS[slot])

    to_par = [
        remote(src, dst, par_send, par_recv, k, par)
        for k, (src, dst) in enumerate(zip(mine + pieces, small(2) + landed(2)))
    ]
    to_sib = [
        remote(src, dst, sib_send, sib_recv, k, sib)
        for k, (src, dst) in enumerate(zip(mine + (cl_hbm.at[0],), small(1) + landed(1)))
    ]
    forward = [
        remote(src, dst, fwd_send, fwd_recv, k, sib)
        for k, (src, dst) in enumerate(zip(small(2) + landed(2)[:RELAYED], small(3) + landed(3)[:RELAYED]))
    ]
    to_far = remote(pieces[RELAYED], landed(3)[RELAYED], far_send, far_recv, 0, far)
    for copy in to_par[:4] + to_sib + to_par[4:] + [to_far]:
        copy.start()
    loads["wv"].start()

    row_of = lax.broadcasted_iota(jnp.int32, (KEXT - DC - DR, 2 * Q), 0)
    tail = jnp.where(row_of == 0, BLOCKED, 0.0).astype(BF16)
    for pair in range(PAIRS):
        qt[pair, DC + DR :, :] = tail

    loads["wk"].wait()
    loads["qn"].wait()
    loads["qr"].wait()
    for head in range(HERE):
        pair, side = head // 2, (head % 2) * Q
        part = lax.dot_general(
            wk[:, head * DH : (head + 1) * DH], qn[:, head * DH : (head + 1) * DH],
            (((1,), (1,)), ((), ())), preferred_element_type=F32,
        )
        qt[pair, :DC, side : side + Q] = part.astype(BF16)
    for pair in range(PAIRS):
        turned = qr[:, pair * 2 * DR : (pair + 1) * 2 * DR].T
        qt[pair, DC : DC + DR, :Q] = turned[:DR]
        qt[pair, DC : DC + DR, Q:] = turned[DR:]

    lane = lax.broadcasted_iota(jnp.int32, (DR, ROWS), 1)
    row = lax.broadcasted_iota(jnp.int32, (DR, ROWS), 0)

    def prepare_new(slot):
        begin = NEW0 + slot * NEW
        ext[begin : begin + NEW, :] = jnp.concatenate(
            [nrope[slot], jnp.zeros((NEW, KEXT - DC - DR), BF16)], axis=1
        )

    def prepare_cached(slot):
        live = jnp.broadcast_to(lens[slot], (DR, ROWS))
        dead = jnp.where((row == 0) & (lane >= live), 1.0, 0.0).astype(BF16)
        wide = jnp.concatenate([rope[slot], dead], axis=0).T
        for begin, first, count in SLOT_ROWS[slot]:
            ext[begin : begin + count, :] = wide[first : first + count]

    def turn(begin, count, column, columns):
        rows = lat[begin : begin + count, :]
        if columns > count:
            rows = jnp.concatenate([rows, jnp.zeros((columns - count, DC), BF16)], axis=0)
        latt[:, column : column + columns] = rows.T

    local_row = lax.broadcasted_iota(jnp.int32, (CTX * NEW, 2 * Q), 0)
    query = lax.rem(lax.broadcasted_iota(jnp.int32, (CTX * NEW, 2 * Q), 1), Q)
    slot_of = lax.div(local_row, NEW)
    owner = jnp.where(
        slot_of == 0, me, jnp.where(slot_of == 1, sib, jnp.where(slot_of == 2, par, far))
    )
    fresh = owner * NEW + lax.rem(local_row, NEW) <= query

    score, weight, factor = (score0, score1), (weight0, weight1), (factor0, factor1)
    items = [(chunk, pair) for chunk in range(len(CHUNKS)) for pair in range(PAIRS)]

    def score_of(index):
        chunk, pair = items[index]
        begin, count = CHUNKS[chunk][:2]
        keys = jnp.concatenate(
            [lat[begin : begin + count, :], ext[begin : begin + count, :]], axis=1
        )
        score[index % 2][:count] = jnp.dot(keys, qt[pair], preferred_element_type=F32)

    def weigh(index):
        chunk, pair = items[index]
        begin, count, _, columns = CHUNKS[chunk]
        scores = score[index % 2][:count]
        if begin == NEW0:
            new = CTX * NEW
            scores = jnp.concatenate([jnp.where(fresh, scores[:new], BLOCKED), scores[new:]], axis=0)
        level = jnp.max(scores, axis=0, keepdims=True)
        if chunk:
            level = jnp.maximum(top[pair], level)
            change = jnp.exp2((top[pair] - level) * SCALE)
            factor[index % 2][...] = change
        weights = jnp.exp2((scores - level) * SCALE)
        sums = jnp.sum(weights, axis=0, keepdims=True)
        top[pair] = level
        total[pair] = total[pair] * change + sums if chunk else sums
        weights = weights.astype(BF16)
        if columns > count:
            weights = jnp.concatenate([weights, jnp.zeros((columns - count, 2 * Q), BF16)], axis=0)
        weight[index % 2][:columns] = weights

    def gather_in(index):
        chunk, pair = items[index]
        _, _, column, columns = CHUNKS[chunk]
        part = jnp.dot(
            latt[:, column : column + columns],
            weight[index % 2][:columns],
            preferred_element_type=F32,
        )
        acc[pair] = acc[pair] * factor[index % 2][...] + part if chunk else part

    def finish(index):
        pair = items[index][1]
        mean = (acc[pair] * (1.0 / total[pair])).astype(BF16)
        for side in range(2):
            head = 2 * pair + side
            out[0, :, head * DV : (head + 1) * DV] = lax.dot_general(
                mean[:, side * Q : (side + 1) * Q], wv[:, head * DV : (head + 1) * DV],
                (((0,), (0,)), ((), ())), preferred_element_type=F32,
            ).astype(BF16)

    def onward(indices):
        for k in indices:
            to_par[k].wait_recv()
            forward[k].start()

    def before_item(index):
        if index == 0:
            for name in ("cl", "cr", "nl", "nr", "ln"):
                loads[name].wait()
            for copy in to_sib:
                copy.wait_recv()
            for slot in range(2):
                prepare_new(slot)
                prepare_cached(slot)
            turn(*CHUNKS[0])
        if index == 5:
            onward(range(4))
        if index == PAIRS:
            onward(range(4, 5))
            for copy in forward[:4]:
                copy.wait_recv()
            for slot in range(2, 4):
                prepare_new(slot)
                prepare_cached(slot)
            turn(*CHUNKS[1])
        if index == 2 * PAIRS:
            onward(range(5, 6))
            forward[4].wait_recv()
            turn(*CHUNKS[2])
        if index == 3 * PAIRS:
            loads["wv"].wait()
            forward[5].wait_recv()
            to_par[6].wait_recv()
            to_far.wait_recv()
            turn(*CHUNKS[3])

    stages = (score_of, weigh, gather_in)
    done = [0, 0, 0]

    def advance(stage, index):
        if done[stage] <= index < len(items):
            assert done[stage] == index
            done[stage] += 1
            stages[stage](index)

    last = len(items) - PAIRS
    for index in range(len(items) + 3):
        if index in (PAIRS, 2 * PAIRS):
            advance(1, index - 1)
            advance(2, index - 2)
            advance(2, index - 1)
        before_item(index)
        advance(0, index)
        if index >= 1:
            advance(1, index - 1)
        if index >= 2:
            advance(2, index - 2)
        if index >= last + 3:
            finish(index - 3)
    for copy in to_par + to_sib + forward + [to_far]:
        copy.wait_send()


def shards(*operands):
    operands = operands[:3] + (jnp.swapaxes(operands[3], 1, 2),) + operands[4:]
    operands = tuple(
        x if index == 6 else pltpu.with_memory_space_constraint(x, pltpu.HBM)
        for index, x in enumerate(operands)
    )
    return pl.pallas_call(
        kernel,
        out_shape=pltpu.VMEM((1, Q, HERE * DV), BF16),
        in_specs=[pl.BlockSpec(memory_space=pltpu.HBM)] * 9,
        out_specs=pl.BlockSpec(memory_space=pltpu.VMEM),
        scratch_shapes=[
            pltpu.VMEM((Q, HERE * DH), BF16),
            pltpu.VMEM((Q, HERE * DR), BF16),
            pltpu.VMEM((DC, HERE * DH), BF16),
            pltpu.VMEM((DC, HERE * DV), BF16),
            pltpu.VMEM((NROW, DC), BF16),
            pltpu.VMEM((CTX, DR, ROWS), BF16),
            pltpu.VMEM((CTX, NEW, DR), BF16),
            pltpu.VMEM((CTX, 1, 1), jnp.int32),
            pltpu.VMEM((NROW, KEXT - DC), BF16),
            pltpu.VMEM((DC, TURNED), BF16),
            pltpu.VMEM((PAIRS, KEXT, 2 * Q), BF16),
            pltpu.VMEM((PAIRS, DC, 2 * Q), F32),
            pltpu.VMEM((PAIRS, 1, 2 * Q), F32),
            pltpu.VMEM((PAIRS, 1, 2 * Q), F32),
            pltpu.VMEM((2 * ROWS, 2 * Q), F32),
            pltpu.VMEM((2 * ROWS, 2 * Q), F32),
            pltpu.VMEM((2 * ROWS, 2 * Q), BF16),
            pltpu.VMEM((2 * ROWS, 2 * Q), BF16),
            pltpu.VMEM((1, 2 * Q), F32),
            pltpu.VMEM((1, 2 * Q), F32),
            pltpu.SemaphoreType.DMA((9,)),
        ]
        + [pltpu.SemaphoreType.DMA((7,))] * 6
        + [pltpu.SemaphoreType.DMA((1,))] * 2,
        compiler_params=pltpu.CompilerParams(
            collective_id=0, has_side_effects=True, vmem_limit_bytes=40 << 20
        ),
        cost_estimate=pl.CostEstimate(
            flops=7_000_000_000, bytes_accessed=7_000_000, transcendentals=2_400_000
        ),
        name="latent_attention",
    )(*operands)


def solution(mesh):
    return jax.shard_map(
        shards,
        mesh=mesh,
        in_specs=(
            P("req", None, None),
            P("req", None, None),
            P("req", "ctx", None),
            P("req", "ctx", None),
            P("req", "ctx", None),
            P("req", "ctx", None),
            P("req", "ctx"),
            P(None, "ctx"),
            P(None, "ctx"),
        ),
        out_specs=P("req", None, "ctx"),
        check_vma=False,
    )
```

```python
import functools
import math

import jax
import jax.numpy as jnp
from jax import lax
from jax.experimental import pallas as pl
from jax.experimental.pallas import tpu as pltpu
from jax.sharding import PartitionSpec as P

DC = 512
DR = 64
DH = 128
DV = 128
HEADS = 64
CTX = 4
HERE = HEADS // CTX
PAIRS = HERE // 2
Q = 128
ROWS = 256
NEW = 32
NROW = CTX * (ROWS + NEW)
KEXT = DC + 128
LOG2E = 1.4426950408889634
SCALE = LOG2E / math.sqrt(DH + DR)
BLOCKED = -1e30
MESH = pl.DeviceIdType.MESH
F32 = jnp.float32
BF16 = jnp.bfloat16

PIECES = (128, 80, 48)
STARTS = (0, 128, 208)
RELAYED = 2
NEW0 = 2 * ROWS
FAR0 = NEW0 + CTX * NEW
LANDS = (
    None,
    (ROWS,),
    (FAR0, FAR0 + 2 * PIECES[0], FAR0 + 2 * PIECES[0] + 2 * PIECES[1]),
    (FAR0 + PIECES[0], FAR0 + 2 * PIECES[0] + PIECES[1], FAR0 + 2 * PIECES[0] + 2 * PIECES[1] + PIECES[2]),
)
SLOT_ROWS = (
    ((0, 0, ROWS),),
    ((ROWS, 0, ROWS),),
    tuple(zip(LANDS[2], STARTS, PIECES)),
    tuple(zip(LANDS[3], STARTS, PIECES)),
)
CHUNKS = (
    (0, 2 * ROWS, 0, 2 * ROWS),
    (NEW0, CTX * NEW + PIECES[0], 512, 256),
    (LANDS[3][0], PIECES[0] + PIECES[1], 768, 256),
    (LANDS[3][1], PIECES[1] + 2 * PIECES[2], 1024, 256),
)
TURNED = 1280


def kernel(
    qn_hbm, qr_hbm, cl_hbm, cr_hbm, nl_hbm, nr_hbm, len_hbm, wk_hbm, wv_hbm, out,
    qn, qr, wk, wv, lat, rope, nrope, lens, ext, latt, qt, acc, top, total,
    score0, score1, weight0, weight1, factor0, factor1,
    load_sem, sib_send, sib_recv, par_send, par_recv, fwd_send, fwd_recv, far_send, far_recv,
):
    me = lax.axis_index("ctx")
    sib = me + 1 - 2 * lax.rem(me, 2)
    par = lax.rem(me + 2, CTX)
    far = lax.rem(sib + 2, CTX)

    def local(index, src, dst):
        return pltpu.make_async_copy(src, dst, load_sem.at[index])

    loads = dict(
        wk=local(0, wk_hbm, wk),
        qn=local(1, qn_hbm.at[0, :, pl.ds(pl.multiple_of(me * HERE * DH, HERE * DH), HERE * DH)], qn),
        qr=local(2, qr_hbm.at[0, :, pl.ds(pl.multiple_of(me * HERE * DR, HERE * DR), HERE * DR)], qr),
        cl=local(3, cl_hbm.at[0], lat.at[pl.ds(0, ROWS)]),
        cr=local(4, cr_hbm.at[0], rope.at[0]),
        nl=local(5, nl_hbm.at[0], lat.at[pl.ds(NEW0, NEW)]),
        nr=local(6, nr_hbm.at[0], nrope.at[0]),
        ln=local(7, len_hbm, lens.at[0]),
        wv=local(8, wv_hbm, wv),
    )
    barrier = pltpu.get_barrier_semaphore()
    for peer in (sib, par, far):
        pl.semaphore_signal(barrier, inc=1, device_id={"ctx": peer}, device_id_type=MESH)
    for name in ("wk", "qn", "qr", "cl", "cr", "nl", "nr", "ln"):
        loads[name].start()
    pl.semaphore_wait(barrier, 3)

    def remote(src, dst, send, recv, index, peer):
        return pltpu.make_async_remote_copy(
            src_ref=src, dst_ref=dst, send_sem=send.at[index], recv_sem=recv.at[index],
            device_id={"ctx": peer}, device_id_type=MESH,
        )

    def small(slot):
        return (
            nrope.at[slot], lat.at[pl.ds(NEW0 + slot * NEW, NEW)], lens.at[slot], rope.at[slot],
        )

    mine = (nr_hbm.at[0], nl_hbm.at[0], len_hbm, cr_hbm.at[0])
    pieces = tuple(cl_hbm.at[0, pl.ds(start, count)] for start, count in zip(STARTS, PIECES))

    def landed(slot):
        return tuple(lat.at[pl.ds(row, count)] for row, _, count in SLOT_ROWS[slot])

    to_par = [
        remote(src, dst, par_send, par_recv, k, par)
        for k, (src, dst) in enumerate(zip(mine + pieces, small(2) + landed(2)))
    ]
    to_sib = [
        remote(src, dst, sib_send, sib_recv, k, sib)
        for k, (src, dst) in enumerate(zip(mine + (cl_hbm.at[0],), small(1) + landed(1)))
    ]
    forward = [
        remote(src, dst, fwd_send, fwd_recv, k, sib)
        for k, (src, dst) in enumerate(zip(small(2) + landed(2)[:RELAYED], small(3) + landed(3)[:RELAYED]))
    ]
    to_far = remote(pieces[RELAYED], landed(3)[RELAYED], far_send, far_recv, 0, far)
    for copy in to_par[:5] + to_sib:
        copy.start()
    loads["wv"].start()

    row_of = lax.broadcasted_iota(jnp.int32, (KEXT - DC - DR, 2 * Q), 0)
    tail = jnp.where(row_of == 0, BLOCKED, 0.0).astype(BF16)
    for pair in range(PAIRS):
        qt[pair, DC + DR :, :] = tail

    loads["wk"].wait()
    loads["qn"].wait()
    loads["qr"].wait()
    for head in range(HERE):
        pair, side = head // 2, (head % 2) * Q
        part = lax.dot_general(
            wk[:, head * DH : (head + 1) * DH], qn[:, head * DH : (head + 1) * DH],
            (((1,), (1,)), ((), ())), preferred_element_type=F32,
        )
        qt[pair, :DC, side : side + Q] = part.astype(BF16)
    for pair in range(PAIRS):
        turned = qr[:, pair * 2 * DR : (pair + 1) * 2 * DR].T
        qt[pair, DC : DC + DR, :Q] = turned[:DR]
        qt[pair, DC : DC + DR, Q:] = turned[DR:]

    lane = lax.broadcasted_iota(jnp.int32, (DR, ROWS), 1)
    row = lax.broadcasted_iota(jnp.int32, (DR, ROWS), 0)

    def prepare_new(slot):
        begin = NEW0 + slot * NEW
        ext[begin : begin + NEW, :] = jnp.concatenate(
            [nrope[slot], jnp.zeros((NEW, KEXT - DC - DR), BF16)], axis=1
        )

    def prepare_cached(slot):
        live = jnp.broadcast_to(lens[slot], (DR, ROWS))
        dead = jnp.where((row == 0) & (lane >= live), 1.0, 0.0).astype(BF16)
        wide = jnp.concatenate([rope[slot], dead], axis=0).T
        for begin, first, count in SLOT_ROWS[slot]:
            ext[begin : begin + count, :] = wide[first : first + count]

    def turn(begin, count, column, columns):
        rows = lat[begin : begin + count, :]
        if columns > count:
            rows = jnp.concatenate([rows, jnp.zeros((columns - count, DC), BF16)], axis=0)
        latt[:, column : column + columns] = rows.T

    local_row = lax.broadcasted_iota(jnp.int32, (CTX * NEW, 2 * Q), 0)
    query = lax.rem(lax.broadcasted_iota(jnp.int32, (CTX * NEW, 2 * Q), 1), Q)
    slot_of = lax.div(local_row, NEW)
    owner = jnp.where(
        slot_of == 0, me, jnp.where(slot_of == 1, sib, jnp.where(slot_of == 2, par, far))
    )
    fresh = owner * NEW + lax.rem(local_row, NEW) <= query

    score, weight, factor = (score0, score1), (weight0, weight1), (factor0, factor1)
    items = [(chunk, pair) for chunk in range(len(CHUNKS)) for pair in range(PAIRS)]

    def score_of(index):
        chunk, pair = items[index]
        begin, count = CHUNKS[chunk][:2]
        keys = jnp.concatenate(
            [lat[begin : begin + count, :], ext[begin : begin + count, :]], axis=1
        )
        score[index % 2][:count] = jnp.dot(keys, qt[pair], preferred_element_type=F32)

    def weigh(index):
        chunk, pair = items[index]
        begin, count, _, columns = CHUNKS[chunk]
        scores = score[index % 2][:count]
        if begin == NEW0:
            new = CTX * NEW
            scores = jnp.concatenate([jnp.where(fresh, scores[:new], BLOCKED), scores[new:]], axis=0)
        level = jnp.max(scores, axis=0, keepdims=True)
        if chunk:
            level = jnp.maximum(top[pair], level)
            change = jnp.exp2((top[pair] - level) * SCALE)
            factor[index % 2][...] = change
        weights = jnp.exp2((scores - level) * SCALE)
        sums = jnp.sum(weights, axis=0, keepdims=True)
        top[pair] = level
        total[pair] = total[pair] * change + sums if chunk else sums
        weights = weights.astype(BF16)
        if columns > count:
            weights = jnp.concatenate([weights, jnp.zeros((columns - count, 2 * Q), BF16)], axis=0)
        weight[index % 2][:columns] = weights

    def gather_in(index):
        chunk, pair = items[index]
        _, _, column, columns = CHUNKS[chunk]
        part = jnp.dot(
            latt[:, column : column + columns],
            weight[index % 2][:columns],
            preferred_element_type=F32,
        )
        acc[pair] = acc[pair] * factor[index % 2][...] + part if chunk else part

    def finish(index):
        pair = items[index][1]
        mean = (acc[pair] * (1.0 / total[pair])).astype(BF16)
        for side in range(2):
            head = 2 * pair + side
            out[0, :, head * DV : (head + 1) * DV] = lax.dot_general(
                mean[:, side * Q : (side + 1) * Q], wv[:, head * DV : (head + 1) * DV],
                (((0,), (0,)), ((), ())), preferred_element_type=F32,
            ).astype(BF16)

    def onward(indices):
        for k in indices:
            to_par[k].wait_recv()
            forward[k].start()

    def before_item(index):
        if index == 0:
            for name in ("cl", "cr", "nl", "nr", "ln"):
                loads[name].wait()
            for copy in to_sib:
                copy.wait_recv()
            for slot in range(2):
                prepare_new(slot)
                prepare_cached(slot)
            turn(*CHUNKS[0])
        if index == PAIRS - 2:
            to_par[5].start()
        if index == PAIRS:
            onward(range(4))
            to_par[5].wait_send()
            to_par[6].start()
            to_far.start()
            onward(range(4, 5))
            for copy in forward[:4]:
                copy.wait_recv()
            for slot in range(2, 4):
                prepare_new(slot)
                prepare_cached(slot)
            turn(*CHUNKS[1])
        if index == 2 * PAIRS:
            onward(range(5, 6))
            forward[4].wait_recv()
            turn(*CHUNKS[2])
        if index == 3 * PAIRS:
            loads["wv"].wait()
            forward[5].wait_recv()
            to_par[6].wait_recv()
            to_far.wait_recv()
            turn(*CHUNKS[3])

    stages = (score_of, weigh, gather_in)
    done = [0, 0, 0]

    def advance(stage, index):
        if done[stage] <= index < len(items):
            assert done[stage] == index
            done[stage] += 1
            stages[stage](index)

    last = len(items) - PAIRS
    for index in range(len(items) + 3):
        if index in (PAIRS, 2 * PAIRS, 3 * PAIRS):
            advance(1, index - 1)
            advance(2, index - 2)
            advance(2, index - 1)
        before_item(index)
        advance(0, index)
        if index >= 1:
            advance(1, index - 1)
        if index >= 2:
            advance(2, index - 2)
        if index >= last + 3:
            finish(index - 3)
    for copy in to_par[:5] + to_par[6:] + to_sib + forward + [to_far]:
        copy.wait_send()


def shards(*operands):
    operands = operands[:3] + (jnp.swapaxes(operands[3], 1, 2),) + operands[4:]
    operands = tuple(
        x if index == 6 else pltpu.with_memory_space_constraint(x, pltpu.HBM)
        for index, x in enumerate(operands)
    )
    return pl.pallas_call(
        kernel,
        out_shape=pltpu.VMEM((1, Q, HERE * DV), BF16),
        in_specs=[pl.BlockSpec(memory_space=pltpu.HBM)] * 9,
        out_specs=pl.BlockSpec(memory_space=pltpu.VMEM),
        scratch_shapes=[
            pltpu.VMEM((Q, HERE * DH), BF16),
            pltpu.VMEM((Q, HERE * DR), BF16),
            pltpu.VMEM((DC, HERE * DH), BF16),
            pltpu.VMEM((DC, HERE * DV), BF16),
            pltpu.VMEM((NROW, DC), BF16),
            pltpu.VMEM((CTX, DR, ROWS), BF16),
            pltpu.VMEM((CTX, NEW, DR), BF16),
            pltpu.VMEM((CTX, 1, 1), jnp.int32),
            pltpu.VMEM((NROW, KEXT - DC), BF16),
            pltpu.VMEM((DC, TURNED), BF16),
            pltpu.VMEM((PAIRS, KEXT, 2 * Q), BF16),
            pltpu.VMEM((PAIRS, DC, 2 * Q), F32),
            pltpu.VMEM((PAIRS, 1, 2 * Q), F32),
            pltpu.VMEM((PAIRS, 1, 2 * Q), F32),
            pltpu.VMEM((2 * ROWS, 2 * Q), F32),
            pltpu.VMEM((2 * ROWS, 2 * Q), F32),
            pltpu.VMEM((2 * ROWS, 2 * Q), BF16),
            pltpu.VMEM((2 * ROWS, 2 * Q), BF16),
            pltpu.VMEM((1, 2 * Q), F32),
            pltpu.VMEM((1, 2 * Q), F32),
            pltpu.SemaphoreType.DMA((9,)),
        ]
        + [pltpu.SemaphoreType.DMA((7,))] * 6
        + [pltpu.SemaphoreType.DMA((1,))] * 2,
        compiler_params=pltpu.CompilerParams(
            collective_id=0, has_side_effects=True, vmem_limit_bytes=40 << 20
        ),
        cost_estimate=pl.CostEstimate(
            flops=7_000_000_000, bytes_accessed=7_000_000, transcendentals=2_400_000
        ),
        name="latent_attention",
    )(*operands)


def solution(mesh):
    return jax.shard_map(
        shards,
        mesh=mesh,
        in_specs=(
            P("req", None, None),
            P("req", None, None),
            P("req", "ctx", None),
            P("req", "ctx", None),
            P("req", "ctx", None),
            P("req", "ctx", None),
            P("req", "ctx"),
            P(None, "ctx"),
            P(None, "ctx"),
        ),
        out_specs=P("req", None, "ctx"),
        check_vma=False,
    )
```

```python
import functools
import math

import jax
import jax.numpy as jnp
from jax import lax
from jax.experimental import pallas as pl
from jax.experimental.pallas import tpu as pltpu
from jax.sharding import PartitionSpec as P

DC = 512
DR = 64
DH = 128
DV = 128
HEADS = 64
CTX = 4
HERE = HEADS // CTX
PAIRS = HERE // 2
Q = 128
ROWS = 256
NEW = 32
NROW = CTX * (ROWS + NEW)
KEXT = DC + 128
LOG2E = 1.4426950408889634
SCALE = LOG2E / math.sqrt(DH + DR)
BLOCKED = -1e30
MESH = pl.DeviceIdType.MESH
F32 = jnp.float32
BF16 = jnp.bfloat16

PIECES = (128, 80, 48)
STARTS = (0, 128, 208)
RELAYED = 2
NEAR0 = 2 * ROWS
FAR0 = NEAR0 + 3 * NEW + PIECES[0]
LAST0 = FAR0 + NEW + PIECES[0] + PIECES[1]
NEWS = (NEAR0, NEAR0 + NEW, NEAR0 + 2 * NEW, FAR0)
LANDS = (
    None,
    (ROWS,),
    (NEAR0 + 3 * NEW, LAST0 - PIECES[1], LAST0 + PIECES[1]),
    (FAR0 + NEW, LAST0, LAST0 + PIECES[1] + PIECES[2]),
)
SLOT_ROWS = (
    ((0, 0, ROWS),),
    ((ROWS, 0, ROWS),),
    tuple(zip(LANDS[2], STARTS, PIECES)),
    tuple(zip(LANDS[3], STARTS, PIECES)),
)
CHUNKS = (
    (0, ROWS, 0, ROWS),
    (ROWS, ROWS, ROWS, ROWS),
    (NEAR0, FAR0 - NEAR0, 512, 256),
    (FAR0, LAST0 - FAR0, 768, 256),
    (LAST0, NROW - LAST0, 1024, 256),
)
TURNED = 1280


def kernel(
    qn_hbm, qr_hbm, cl_hbm, cr_hbm, nl_hbm, nr_hbm, len_hbm, wk_hbm, wv_hbm, out,
    qn, qr, wk, wv, lat, rope, nrope, lens, ext, latt, qt, acc, top, total,
    score0, score1, weight0, weight1, factor0, factor1,
    load_sem, sib_send, sib_recv, par_send, par_recv, fwd_send, fwd_recv, far_send, far_recv,
):
    me = lax.axis_index("ctx")
    sib = me + 1 - 2 * lax.rem(me, 2)
    par = lax.rem(me + 2, CTX)
    far = lax.rem(sib + 2, CTX)

    def local(index, src, dst):
        return pltpu.make_async_copy(src, dst, load_sem.at[index])

    loads = dict(
        wk=local(0, wk_hbm, wk),
        qn=local(1, qn_hbm.at[0, :, pl.ds(pl.multiple_of(me * HERE * DH, HERE * DH), HERE * DH)], qn),
        qr=local(2, qr_hbm.at[0, :, pl.ds(pl.multiple_of(me * HERE * DR, HERE * DR), HERE * DR)], qr),
        cl=local(3, cl_hbm.at[0], lat.at[pl.ds(0, ROWS)]),
        cr=local(4, cr_hbm.at[0], rope.at[0]),
        nl=local(5, nl_hbm.at[0], lat.at[pl.ds(NEWS[0], NEW)]),
        nr=local(6, nr_hbm.at[0], nrope.at[0]),
        ln=local(7, len_hbm, lens.at[0]),
        wv=local(8, wv_hbm, wv),
    )
    barrier = pltpu.get_barrier_semaphore()
    for peer in (sib, par, far):
        pl.semaphore_signal(barrier, inc=1, device_id={"ctx": peer}, device_id_type=MESH)
    for name in ("wk", "qn", "qr", "cl", "cr", "nl", "nr", "ln"):
        loads[name].start()
    pl.semaphore_wait(barrier, 3)

    def remote(src, dst, send, recv, index, peer):
        return pltpu.make_async_remote_copy(
            src_ref=src, dst_ref=dst, send_sem=send.at[index], recv_sem=recv.at[index],
            device_id={"ctx": peer}, device_id_type=MESH,
        )

    def small(slot):
        return (
            nrope.at[slot], lat.at[pl.ds(NEWS[slot], NEW)], lens.at[slot], rope.at[slot],
        )

    mine = (nr_hbm.at[0], nl_hbm.at[0], len_hbm, cr_hbm.at[0])
    pieces = tuple(cl_hbm.at[0, pl.ds(start, count)] for start, count in zip(STARTS, PIECES))

    def landed(slot):
        return tuple(lat.at[pl.ds(row, count)] for row, _, count in SLOT_ROWS[slot])

    to_par = [
        remote(src, dst, par_send, par_recv, k, par)
        for k, (src, dst) in enumerate(zip(mine + pieces, small(2) + landed(2)))
    ]
    to_sib = [
        remote(src, dst, sib_send, sib_recv, k, sib)
        for k, (src, dst) in enumerate(zip(mine + (cl_hbm.at[0],), small(1) + landed(1)))
    ]
    forward = [
        remote(src, dst, fwd_send, fwd_recv, k, sib)
        for k, (src, dst) in enumerate(zip(small(2) + landed(2)[:RELAYED], small(3) + landed(3)[:RELAYED]))
    ]
    to_far = remote(pieces[RELAYED], landed(3)[RELAYED], far_send, far_recv, 0, far)
    for copy in to_par[:4] + to_sib:
        copy.start()

    row_of = lax.broadcasted_iota(jnp.int32, (KEXT - DC - DR, 2 * Q), 0)
    tail = jnp.where(row_of == 0, BLOCKED, 0.0).astype(BF16)
    for pair in range(PAIRS):
        qt[pair, DC + DR :, :] = tail

    loads["wk"].wait()
    loads["qn"].wait()
    loads["qr"].wait()
    to_par[4].start()
    loads["wv"].start()
    for head in range(HERE):
        pair, side = head // 2, (head % 2) * Q
        part = lax.dot_general(
            wk[:, head * DH : (head + 1) * DH], qn[:, head * DH : (head + 1) * DH],
            (((1,), (1,)), ((), ())), preferred_element_type=F32,
        )
        qt[pair, :DC, side : side + Q] = part.astype(BF16)
    for pair in range(PAIRS):
        turned = qr[:, pair * 2 * DR : (pair + 1) * 2 * DR].T
        qt[pair, DC : DC + DR, :Q] = turned[:DR]
        qt[pair, DC : DC + DR, Q:] = turned[DR:]

    lane = lax.broadcasted_iota(jnp.int32, (DR, ROWS), 1)
    row = lax.broadcasted_iota(jnp.int32, (DR, ROWS), 0)

    def prepare_new(slot):
        begin = NEWS[slot]
        ext[begin : begin + NEW, :] = jnp.concatenate(
            [nrope[slot], jnp.zeros((NEW, KEXT - DC - DR), BF16)], axis=1
        )

    def prepare_cached(slot):
        live = jnp.broadcast_to(lens[slot], (DR, ROWS))
        dead = jnp.where((row == 0) & (lane >= live), 1.0, 0.0).astype(BF16)
        wide = jnp.concatenate([rope[slot], dead], axis=0).T
        for begin, first, count in SLOT_ROWS[slot]:
            ext[begin : begin + count, :] = wide[first : first + count]

    def turn(begin, count, column, columns):
        rows = lat[begin : begin + count, :]
        if columns > count:
            rows = jnp.concatenate([rows, jnp.zeros((columns - count, DC), BF16)], axis=0)
        latt[:, column : column + columns] = rows.T

    local_row = lax.broadcasted_iota(jnp.int32, (CTX * NEW, 2 * Q), 0)
    query = lax.rem(lax.broadcasted_iota(jnp.int32, (CTX * NEW, 2 * Q), 1), Q)
    slot_of = lax.div(local_row, NEW)
    owner = jnp.where(
        slot_of == 0, me, jnp.where(slot_of == 1, sib, jnp.where(slot_of == 2, par, far))
    )
    fresh = owner * NEW + lax.rem(local_row, NEW) <= query

    score, weight, factor = (score0, score1), (weight0, weight1), (factor0, factor1)
    items = [(chunk, pair) for chunk in range(len(CHUNKS)) for pair in range(PAIRS)]

    def score_of(index):
        chunk, pair = items[index]
        begin, count = CHUNKS[chunk][:2]
        keys = jnp.concatenate(
            [lat[begin : begin + count, :], ext[begin : begin + count, :]], axis=1
        )
        score[index % 2][:count] = jnp.dot(keys, qt[pair], preferred_element_type=F32)

    def weigh(index):
        chunk, pair = items[index]
        begin, count, _, columns = CHUNKS[chunk]
        scores = score[index % 2][:count]
        if begin in (NEAR0, FAR0):
            new = 3 * NEW if begin == NEAR0 else NEW
            seen = fresh[: 3 * NEW] if begin == NEAR0 else fresh[3 * NEW :]
            scores = jnp.concatenate([jnp.where(seen, scores[:new], BLOCKED), scores[new:]], axis=0)
        level = jnp.max(scores, axis=0, keepdims=True)
        if chunk:
            level = jnp.maximum(top[pair], level)
            change = jnp.exp2((top[pair] - level) * SCALE)
            factor[index % 2][...] = change
        weights = jnp.exp2((scores - level) * SCALE)
        sums = jnp.sum(weights, axis=0, keepdims=True)
        top[pair] = level
        total[pair] = total[pair] * change + sums if chunk else sums
        weights = weights.astype(BF16)
        if columns > count:
            weights = jnp.concatenate([weights, jnp.zeros((columns - count, 2 * Q), BF16)], axis=0)
        weight[index % 2][:columns] = weights

    def gather_in(index):
        chunk, pair = items[index]
        _, _, column, columns = CHUNKS[chunk]
        part = jnp.dot(
            latt[:, column : column + columns],
            weight[index % 2][:columns],
            preferred_element_type=F32,
        )
        acc[pair] = acc[pair] * factor[index % 2][...] + part if chunk else part

    def finish(index):
        pair = items[index][1]
        mean = (acc[pair] * (1.0 / total[pair])).astype(BF16)
        for side in range(2):
            head = 2 * pair + side
            out[0, :, head * DV : (head + 1) * DV] = lax.dot_general(
                mean[:, side * Q : (side + 1) * Q], wv[:, head * DV : (head + 1) * DV],
                (((0,), (0,)), ((), ())), preferred_element_type=F32,
            ).astype(BF16)

    def onward(indices):
        for k in indices:
            to_par[k].wait_recv()
            forward[k].start()

    def before_item(index):
        if index == 0:
            for name in ("cl", "cr", "nl", "nr", "ln"):
                loads[name].wait()
            prepare_new(0)
            prepare_cached(0)
            turn(*CHUNKS[0])
        if index == PAIRS - 1:
            to_par[5].start()
        if index == PAIRS:
            for copy in to_sib:
                copy.wait_recv()
            prepare_new(1)
            prepare_cached(1)
            turn(*CHUNKS[1])
        if index == 2 * PAIRS - 3:
            to_par[6].start()
            to_far.start()
        if index == 2 * PAIRS - 1:
            onward(range(4))
        if index == 2 * PAIRS:
            onward(range(4, 5))
            prepare_new(2)
            prepare_cached(2)
            turn(*CHUNKS[2])
        if index == 3 * PAIRS:
            onward(range(5, 6))
            for copy in forward[:5]:
                copy.wait_recv()
            prepare_new(3)
            prepare_cached(3)
            turn(*CHUNKS[3])
        if index == 4 * PAIRS:
            loads["wv"].wait()
            forward[5].wait_recv()
            to_par[6].wait_recv()
            to_far.wait_recv()
            turn(*CHUNKS[4])

    stages = (score_of, weigh, gather_in)
    done = [0, 0, 0]

    def advance(stage, index):
        if done[stage] <= index < len(items):
            assert done[stage] == index
            done[stage] += 1
            stages[stage](index)

    last = len(items) - PAIRS
    for index in range(len(items) + 3):
        if index in (2 * PAIRS, 3 * PAIRS, 4 * PAIRS):
            advance(1, index - 1)
            advance(2, index - 2)
            advance(2, index - 1)
        before_item(index)
        advance(0, index)
        if index >= 1:
            advance(1, index - 1)
        if index >= 2:
            advance(2, index - 2)
        if index >= last + 3:
            finish(index - 3)
    for copy in to_par + to_sib + forward + [to_far]:
        copy.wait_send()


def shards(*operands):
    operands = operands[:3] + (jnp.swapaxes(operands[3], 1, 2),) + operands[4:]
    operands = tuple(
        x if index == 6 else pltpu.with_memory_space_constraint(x, pltpu.HBM)
        for index, x in enumerate(operands)
    )
    return pl.pallas_call(
        kernel,
        out_shape=pltpu.VMEM((1, Q, HERE * DV), BF16),
        in_specs=[pl.BlockSpec(memory_space=pltpu.HBM)] * 9,
        out_specs=pl.BlockSpec(memory_space=pltpu.VMEM),
        scratch_shapes=[
            pltpu.VMEM((Q, HERE * DH), BF16),
            pltpu.VMEM((Q, HERE * DR), BF16),
            pltpu.VMEM((DC, HERE * DH), BF16),
            pltpu.VMEM((DC, HERE * DV), BF16),
            pltpu.VMEM((NROW, DC), BF16),
            pltpu.VMEM((CTX, DR, ROWS), BF16),
            pltpu.VMEM((CTX, NEW, DR), BF16),
            pltpu.VMEM((CTX, 1, 1), jnp.int32),
            pltpu.VMEM((NROW, KEXT - DC), BF16),
            pltpu.VMEM((DC, TURNED), BF16),
            pltpu.VMEM((PAIRS, KEXT, 2 * Q), BF16),
            pltpu.VMEM((PAIRS, DC, 2 * Q), F32),
            pltpu.VMEM((PAIRS, 1, 2 * Q), F32),
            pltpu.VMEM((PAIRS, 1, 2 * Q), F32),
            pltpu.VMEM((2 * ROWS, 2 * Q), F32),
            pltpu.VMEM((2 * ROWS, 2 * Q), F32),
            pltpu.VMEM((2 * ROWS, 2 * Q), BF16),
            pltpu.VMEM((2 * ROWS, 2 * Q), BF16),
            pltpu.VMEM((1, 2 * Q), F32),
            pltpu.VMEM((1, 2 * Q), F32),
            pltpu.SemaphoreType.DMA((9,)),
        ]
        + [pltpu.SemaphoreType.DMA((7,))] * 6
        + [pltpu.SemaphoreType.DMA((1,))] * 2,
        compiler_params=pltpu.CompilerParams(
            collective_id=0, has_side_effects=True, vmem_limit_bytes=40 << 20
        ),
        cost_estimate=pl.CostEstimate(
            flops=7_000_000_000, bytes_accessed=7_000_000, transcendentals=2_400_000
        ),
        name="latent_attention",
    )(*operands)


def solution(mesh):
    return jax.shard_map(
        shards,
        mesh=mesh,
        in_specs=(
            P("req", None, None),
            P("req", None, None),
            P("req", "ctx", None),
            P("req", "ctx", None),
            P("req", "ctx", None),
            P("req", "ctx", None),
            P("req", "ctx"),
            P(None, "ctx"),
            P(None, "ctx"),
        ),
        out_specs=P("req", None, "ctx"),
        check_vma=False,
    )
```

```python
import functools
import math

import jax
import jax.numpy as jnp
from jax import lax
from jax.experimental import pallas as pl
from jax.experimental.pallas import tpu as pltpu
from jax.sharding import PartitionSpec as P

DC = 512
DR = 64
DH = 128
DV = 128
HEADS = 64
CTX = 4
HERE = HEADS // CTX
PAIRS = HERE // 2
Q = 128
ROWS = 256
NEW = 32
NROW = CTX * (ROWS + NEW)
KEXT = DC + 128
LOG2E = 1.4426950408889634
SCALE = LOG2E / math.sqrt(DH + DR)
BLOCKED = -1e30
MESH = pl.DeviceIdType.MESH
F32 = jnp.float32
BF16 = jnp.bfloat16

PIECES = (128, 80, 48)
STARTS = (0, 128, 208)
RELAYED = 2
NEAR0 = 2 * ROWS
FAR0 = NEAR0 + 2 * NEW + PIECES[0]
LAST0 = FAR0 + NEW + PIECES[0] + PIECES[1]
NEWS = (NEAR0, NEAR0 + NEW, FAR0, LAST0)
LANDS = (
    None,
    (ROWS,),
    (NEAR0 + 2 * NEW, LAST0 - PIECES[1], LAST0 + NEW + PIECES[1]),
    (FAR0 + NEW, LAST0 + NEW, LAST0 + NEW + PIECES[1] + PIECES[2]),
)
FRESH = {NEAR0: (0, 2 * NEW), FAR0: (2 * NEW, 3 * NEW), LAST0: (3 * NEW, 4 * NEW)}
SLOT_ROWS = (
    ((0, 0, ROWS),),
    ((ROWS, 0, ROWS),),
    tuple(zip(LANDS[2], STARTS, PIECES)),
    tuple(zip(LANDS[3], STARTS, PIECES)),
)
CHUNKS = (
    (0, ROWS, 0, ROWS),
    (ROWS, ROWS, ROWS, ROWS),
    (NEAR0, FAR0 - NEAR0, 512, 256),
    (FAR0, LAST0 - FAR0, 768, 256),
    (LAST0, NROW - LAST0, 1024, 256),
)
TURNED = 1280


def kernel(
    qn_hbm, qr_hbm, cl_hbm, cr_hbm, nl_hbm, nr_hbm, len_hbm, wk_hbm, wv_hbm, out,
    qn, qr, wk, wv, lat, rope, nrope, lens, ext, latt, qt, acc, top, total,
    score0, score1, weight0, weight1, factor0, factor1,
    load_sem, sib_send, sib_recv, par_send, par_recv, fwd_send, fwd_recv, far_send, far_recv, ready,
):
    me = lax.axis_index("ctx")
    sib = me + 1 - 2 * lax.rem(me, 2)
    par = lax.rem(me + 2, CTX)
    far = lax.rem(sib + 2, CTX)

    def local(index, src, dst):
        return pltpu.make_async_copy(src, dst, load_sem.at[index])

    loads = dict(
        wk=local(0, wk_hbm, wk),
        qn=local(1, qn_hbm.at[0, :, pl.ds(pl.multiple_of(me * HERE * DH, HERE * DH), HERE * DH)], qn),
        qr=local(2, qr_hbm.at[0, :, pl.ds(pl.multiple_of(me * HERE * DR, HERE * DR), HERE * DR)], qr),
        cl=local(3, cl_hbm.at[0], lat.at[pl.ds(0, ROWS)]),
        cr=local(4, cr_hbm.at[0], rope.at[0]),
        nl=local(5, nl_hbm.at[0], lat.at[pl.ds(NEWS[0], NEW)]),
        nr=local(6, nr_hbm.at[0], nrope.at[0]),
        ln=local(7, len_hbm, lens.at[0]),
        wv=local(8, wv_hbm, wv),
    )
    barrier = pltpu.get_barrier_semaphore()
    for peer in (sib, par):
        pl.semaphore_signal(barrier, inc=1, device_id={"ctx": peer}, device_id_type=MESH)
    for name in ("wk", "qn", "qr", "cl", "cr", "nl", "nr", "ln"):
        loads[name].start()
    pl.semaphore_wait(barrier, 2)
    pl.semaphore_signal(ready, inc=1, device_id={"ctx": sib}, device_id_type=MESH)

    def remote(src, dst, send, recv, index, peer):
        return pltpu.make_async_remote_copy(
            src_ref=src, dst_ref=dst, send_sem=send.at[index], recv_sem=recv.at[index],
            device_id={"ctx": peer}, device_id_type=MESH,
        )

    def small(slot):
        return (
            rope.at[slot], lens.at[slot], nrope.at[slot], lat.at[pl.ds(NEWS[slot], NEW)],
        )

    mine = (cr_hbm.at[0], len_hbm, nr_hbm.at[0], nl_hbm.at[0])
    pieces = tuple(cl_hbm.at[0, pl.ds(start, count)] for start, count in zip(STARTS, PIECES))

    def landed(slot):
        return tuple(lat.at[pl.ds(row, count)] for row, _, count in SLOT_ROWS[slot])

    to_par = [
        remote(src, dst, par_send, par_recv, k, par)
        for k, (src, dst) in enumerate(zip(mine + pieces, small(2) + landed(2)))
    ]
    to_sib = [
        remote(src, dst, sib_send, sib_recv, k, sib)
        for k, (src, dst) in enumerate(zip(mine + (cl_hbm.at[0],), small(1) + landed(1)))
    ]
    forward = [
        remote(src, dst, fwd_send, fwd_recv, k, sib)
        for k, (src, dst) in enumerate(zip(small(2) + landed(2)[:RELAYED], small(3) + landed(3)[:RELAYED]))
    ]
    to_far = remote(pieces[RELAYED], landed(3)[RELAYED], far_send, far_recv, 0, far)
    for copy in to_par[:2] + to_par[4:5] + to_sib:
        copy.start()

    row_of = lax.broadcasted_iota(jnp.int32, (KEXT - DC - DR, 2 * Q), 0)
    tail = jnp.where(row_of == 0, BLOCKED, 0.0).astype(BF16)
    for pair in range(PAIRS):
        qt[pair, DC + DR :, :] = tail

    loads["wk"].wait()
    loads["qn"].wait()
    loads["qr"].wait()
    loads["wv"].start()
    for head in range(HERE):
        pair, side = head // 2, (head % 2) * Q
        part = lax.dot_general(
            wk[:, head * DH : (head + 1) * DH], qn[:, head * DH : (head + 1) * DH],
            (((1,), (1,)), ((), ())), preferred_element_type=F32,
        )
        qt[pair, :DC, side : side + Q] = part.astype(BF16)
    for pair in range(PAIRS):
        turned = qr[:, pair * 2 * DR : (pair + 1) * 2 * DR].T
        qt[pair, DC : DC + DR, :Q] = turned[:DR]
        qt[pair, DC : DC + DR, Q:] = turned[DR:]

    lane = lax.broadcasted_iota(jnp.int32, (DR, ROWS), 1)
    row = lax.broadcasted_iota(jnp.int32, (DR, ROWS), 0)

    def prepare_new(slot):
        begin = NEWS[slot]
        ext[begin : begin + NEW, :] = jnp.concatenate(
            [nrope[slot], jnp.zeros((NEW, KEXT - DC - DR), BF16)], axis=1
        )

    def prepare_cached(slot):
        live = jnp.broadcast_to(lens[slot], (DR, ROWS))
        dead = jnp.where((row == 0) & (lane >= live), 1.0, 0.0).astype(BF16)
        wide = jnp.concatenate([rope[slot], dead], axis=0).T
        for begin, first, count in SLOT_ROWS[slot]:
            ext[begin : begin + count, :] = wide[first : first + count]

    def turn(begin, count, column, columns):
        rows = lat[begin : begin + count, :]
        if columns > count:
            rows = jnp.concatenate([rows, jnp.zeros((columns - count, DC), BF16)], axis=0)
        latt[:, column : column + columns] = rows.T

    local_row = lax.broadcasted_iota(jnp.int32, (CTX * NEW, 2 * Q), 0)
    query = lax.rem(lax.broadcasted_iota(jnp.int32, (CTX * NEW, 2 * Q), 1), Q)
    slot_of = lax.div(local_row, NEW)
    owner = jnp.where(
        slot_of == 0, me, jnp.where(slot_of == 1, sib, jnp.where(slot_of == 2, par, far))
    )
    fresh = owner * NEW + lax.rem(local_row, NEW) <= query

    score, weight, factor = (score0, score1), (weight0, weight1), (factor0, factor1)
    items = [(chunk, pair) for chunk in range(len(CHUNKS)) for pair in range(PAIRS)]

    def score_of(index):
        chunk, pair = items[index]
        begin, count = CHUNKS[chunk][:2]
        keys = jnp.concatenate(
            [lat[begin : begin + count, :], ext[begin : begin + count, :]], axis=1
        )
        score[index % 2][:count] = jnp.dot(keys, qt[pair], preferred_element_type=F32)

    def weigh(index):
        chunk, pair = items[index]
        begin, count, _, columns = CHUNKS[chunk]
        scores = score[index % 2][:count]
        if begin in FRESH:
            lo, hi = FRESH[begin]
            new = hi - lo
            scores = jnp.concatenate(
                [jnp.where(fresh[lo:hi], scores[:new], BLOCKED), scores[new:]], axis=0
            )
        level = jnp.max(scores, axis=0, keepdims=True)
        if chunk:
            level = jnp.maximum(top[pair], level)
            change = jnp.exp2((top[pair] - level) * SCALE)
            factor[index % 2][...] = change
        weights = jnp.exp2((scores - level) * SCALE)
        sums = jnp.sum(weights, axis=0, keepdims=True)
        top[pair] = level
        total[pair] = total[pair] * change + sums if chunk else sums
        weights = weights.astype(BF16)
        if columns > count:
            weights = jnp.concatenate([weights, jnp.zeros((columns - count, 2 * Q), BF16)], axis=0)
        weight[index % 2][:columns] = weights

    def gather_in(index):
        chunk, pair = items[index]
        _, _, column, columns = CHUNKS[chunk]
        part = jnp.dot(
            latt[:, column : column + columns],
            weight[index % 2][:columns],
            preferred_element_type=F32,
        )
        acc[pair] = acc[pair] * factor[index % 2][...] + part if chunk else part

    def finish(index):
        pair = items[index][1]
        mean = (acc[pair] * (1.0 / total[pair])).astype(BF16)
        for side in range(2):
            head = 2 * pair + side
            out[0, :, head * DV : (head + 1) * DV] = lax.dot_general(
                mean[:, side * Q : (side + 1) * Q], wv[:, head * DV : (head + 1) * DV],
                (((0,), (0,)), ((), ())), preferred_element_type=F32,
            ).astype(BF16)

    def onward(indices):
        for k in indices:
            to_par[k].wait_recv()
            forward[k].start()

    def before_item(index):
        if index == 0:
            for name in ("cl", "cr", "nl", "nr", "ln"):
                loads[name].wait()
            prepare_new(0)
            prepare_cached(0)
            turn(*CHUNKS[0])
        if index == PAIRS - 1:
            for k in (2, 3, 5):
                to_par[k].start()
        if index == PAIRS:
            for copy in to_sib:
                copy.wait_recv()
            prepare_new(1)
            prepare_cached(1)
            turn(*CHUNKS[1])
        if index == 2 * PAIRS - 1:
            pl.semaphore_wait(ready, 1)
            to_par[6].start()
            to_far.start()
            onward(range(2))
        if index == 2 * PAIRS:
            onward(range(4, 5))
            prepare_cached(2)
            turn(*CHUNKS[2])
        if index == 3 * PAIRS:
            onward((2, 3, 5))
            for k in (0, 1, 4):
                forward[k].wait_recv()
            prepare_new(2)
            prepare_cached(3)
            turn(*CHUNKS[3])
        if index == 4 * PAIRS:
            loads["wv"].wait()
            for k in (2, 3, 5):
                forward[k].wait_recv()
            to_par[6].wait_recv()
            to_far.wait_recv()
            prepare_new(3)
            turn(*CHUNKS[4])

    stages = (score_of, weigh, gather_in)
    done = [0, 0, 0]

    def advance(stage, index):
        if done[stage] <= index < len(items):
            assert done[stage] == index
            done[stage] += 1
            stages[stage](index)

    last = len(items) - PAIRS
    for index in range(len(items) + 3):
        if index in (2 * PAIRS, 3 * PAIRS):
            advance(1, index - 1)
            advance(2, index - 2)
            advance(2, index - 1)
        before_item(index)
        advance(0, index)
        if index >= 1:
            advance(1, index - 1)
        if index >= 2:
            advance(2, index - 2)
        if index >= last + 3:
            finish(index - 3)
    for copy in to_par + to_sib + forward + [to_far]:
        copy.wait_send()


def shards(*operands):
    operands = operands[:3] + (jnp.swapaxes(operands[3], 1, 2),) + operands[4:]
    operands = tuple(
        x if index == 6 else pltpu.with_memory_space_constraint(x, pltpu.HBM)
        for index, x in enumerate(operands)
    )
    return pl.pallas_call(
        kernel,
        out_shape=pltpu.VMEM((1, Q, HERE * DV), BF16),
        in_specs=[pl.BlockSpec(memory_space=pltpu.HBM)] * 9,
        out_specs=pl.BlockSpec(memory_space=pltpu.VMEM),
        scratch_shapes=[
            pltpu.VMEM((Q, HERE * DH), BF16),
            pltpu.VMEM((Q, HERE * DR), BF16),
            pltpu.VMEM((DC, HERE * DH), BF16),
            pltpu.VMEM((DC, HERE * DV), BF16),
            pltpu.VMEM((NROW, DC), BF16),
            pltpu.VMEM((CTX, DR, ROWS), BF16),
            pltpu.VMEM((CTX, NEW, DR), BF16),
            pltpu.VMEM((CTX, 1, 1), jnp.int32),
            pltpu.VMEM((NROW, KEXT - DC), BF16),
            pltpu.VMEM((DC, TURNED), BF16),
            pltpu.VMEM((PAIRS, KEXT, 2 * Q), BF16),
            pltpu.VMEM((PAIRS, DC, 2 * Q), F32),
            pltpu.VMEM((PAIRS, 1, 2 * Q), F32),
            pltpu.VMEM((PAIRS, 1, 2 * Q), F32),
            pltpu.VMEM((2 * ROWS, 2 * Q), F32),
            pltpu.VMEM((2 * ROWS, 2 * Q), F32),
            pltpu.VMEM((2 * ROWS, 2 * Q), BF16),
            pltpu.VMEM((2 * ROWS, 2 * Q), BF16),
            pltpu.VMEM((1, 2 * Q), F32),
            pltpu.VMEM((1, 2 * Q), F32),
            pltpu.SemaphoreType.DMA((9,)),
        ]
        + [pltpu.SemaphoreType.DMA((7,))] * 6
        + [pltpu.SemaphoreType.DMA((1,))] * 2
        + [pltpu.SemaphoreType.REGULAR],
        compiler_params=pltpu.CompilerParams(
            collective_id=0, has_side_effects=True, vmem_limit_bytes=40 << 20
        ),
        cost_estimate=pl.CostEstimate(
            flops=7_000_000_000, bytes_accessed=7_000_000, transcendentals=2_400_000
        ),
        name="latent_attention",
    )(*operands)


def solution(mesh):
    return jax.shard_map(
        shards,
        mesh=mesh,
        in_specs=(
            P("req", None, None),
            P("req", None, None),
            P("req", "ctx", None),
            P("req", "ctx", None),
            P("req", "ctx", None),
            P("req", "ctx", None),
            P("req", "ctx"),
            P(None, "ctx"),
            P(None, "ctx"),
        ),
        out_specs=P("req", None, "ctx"),
        check_vma=False,
    )
```

```python
import functools
import math

import jax
import jax.numpy as jnp
from jax import lax
from jax.experimental import pallas as pl
from jax.experimental.pallas import tpu as pltpu
from jax.sharding import PartitionSpec as P

DC = 512
DR = 64
DH = 128
DV = 128
HEADS = 64
CTX = 4
HERE = HEADS // CTX
PAIRS = HERE // 2
Q = 128
ROWS = 256
NEW = 32
NROW = CTX * (ROWS + NEW)
KEXT = DC + 128
LOG2E = 1.4426950408889634
SCALE = LOG2E / math.sqrt(DH + DR)
BLOCKED = -1e30
MESH = pl.DeviceIdType.MESH
F32 = jnp.float32
BF16 = jnp.bfloat16

PIECES = (128, 80, 48)
STARTS = (0, 128, 208)
RELAYED = 2
NEAR0 = 2 * ROWS
FAR0 = NEAR0 + 2 * NEW + PIECES[0]
LAST0 = FAR0 + NEW + PIECES[0] + PIECES[1]
NEWS = (NEAR0, NEAR0 + NEW, FAR0, LAST0)
LANDS = (
    None,
    (ROWS,),
    (NEAR0 + 2 * NEW, LAST0 - PIECES[1], LAST0 + NEW + PIECES[1]),
    (FAR0 + NEW, LAST0 + NEW, LAST0 + NEW + PIECES[1] + PIECES[2]),
)
FRESH = {NEAR0: (0, 2 * NEW), FAR0: (2 * NEW, 3 * NEW), LAST0: (3 * NEW, 4 * NEW)}
SLOT_ROWS = (
    ((0, 0, ROWS),),
    ((ROWS, 0, ROWS),),
    tuple(zip(LANDS[2], STARTS, PIECES)),
    tuple(zip(LANDS[3], STARTS, PIECES)),
)
CHUNKS = (
    (0, ROWS, 0, ROWS),
    (ROWS, ROWS, ROWS, ROWS),
    (NEAR0, FAR0 - NEAR0, 512, 256),
    (FAR0, LAST0 - FAR0, 768, 256),
    (LAST0, NROW - LAST0, 1024, 256),
)
TURNED = 1280


def kernel(
    qn_hbm, qr_hbm, cl_hbm, cr_hbm, nl_hbm, nr_hbm, len_hbm, wk_hbm, wv_hbm, out,
    qn, qr, wk, wv, lat, rope, nrope, lens, ext, latt, qt, acc, top, total,
    score0, score1, weight0, weight1, factor0, factor1,
    load_sem, sib_send, sib_recv, par_send, par_recv, fwd_send, fwd_recv, far_send, far_recv, ready,
):
    me = lax.axis_index("ctx")
    sib = me + 1 - 2 * lax.rem(me, 2)
    par = lax.rem(me + 2, CTX)
    far = lax.rem(sib + 2, CTX)

    def local(index, src, dst):
        return pltpu.make_async_copy(src, dst, load_sem.at[index])

    loads = dict(
        wk=local(0, wk_hbm, wk),
        qn=local(1, qn_hbm.at[0, :, pl.ds(pl.multiple_of(me * HERE * DH, HERE * DH), HERE * DH)], qn),
        qr=local(2, qr_hbm.at[0, :, pl.ds(pl.multiple_of(me * HERE * DR, HERE * DR), HERE * DR)], qr),
        cl=local(3, cl_hbm.at[0], lat.at[pl.ds(0, ROWS)]),
        cr=local(4, cr_hbm.at[0], rope.at[0]),
        nl=local(5, nl_hbm.at[0], lat.at[pl.ds(NEWS[0], NEW)]),
        nr=local(6, nr_hbm.at[0], nrope.at[0]),
        ln=local(7, len_hbm, lens.at[0]),
        wv=local(8, wv_hbm, wv),
    )
    barrier = pltpu.get_barrier_semaphore()
    for peer in (sib, par):
        pl.semaphore_signal(barrier, inc=1, device_id={"ctx": peer}, device_id_type=MESH)
    for name in ("wk", "qn", "qr", "cl", "cr", "nl", "nr", "ln"):
        loads[name].start()
    pl.semaphore_wait(barrier, 2)
    pl.semaphore_signal(ready, inc=1, device_id={"ctx": sib}, device_id_type=MESH)

    def remote(src, dst, send, recv, index, peer):
        return pltpu.make_async_remote_copy(
            src_ref=src, dst_ref=dst, send_sem=send.at[index], recv_sem=recv.at[index],
            device_id={"ctx": peer}, device_id_type=MESH,
        )

    def small(slot):
        return (
            rope.at[slot], lens.at[slot], nrope.at[slot], lat.at[pl.ds(NEWS[slot], NEW)],
        )

    mine = (cr_hbm.at[0], len_hbm, nr_hbm.at[0], nl_hbm.at[0])
    pieces = tuple(cl_hbm.at[0, pl.ds(start, count)] for start, count in zip(STARTS, PIECES))

    def landed(slot):
        return tuple(lat.at[pl.ds(row, count)] for row, _, count in SLOT_ROWS[slot])

    to_par = [
        remote(src, dst, par_send, par_recv, k, par)
        for k, (src, dst) in enumerate(zip(mine + pieces, small(2) + landed(2)))
    ]
    to_sib = [
        remote(src, dst, sib_send, sib_recv, k, sib)
        for k, (src, dst) in enumerate(zip(mine + (cl_hbm.at[0],), small(1) + landed(1)))
    ]
    forward = [
        remote(src, dst, fwd_send, fwd_recv, k, sib)
        for k, (src, dst) in enumerate(zip(small(2) + landed(2)[:RELAYED], small(3) + landed(3)[:RELAYED]))
    ]
    to_far = remote(pieces[RELAYED], landed(3)[RELAYED], far_send, far_recv, 0, far)
    for copy in to_par[:2] + to_par[4:5] + to_sib:
        copy.start()

    row_of = lax.broadcasted_iota(jnp.int32, (KEXT - DC - DR, 2 * Q), 0)
    tail = jnp.where(row_of == 0, BLOCKED, 0.0).astype(BF16)
    for pair in range(PAIRS):
        qt[pair, DC + DR :, :] = tail

    loads["wk"].wait()
    loads["qn"].wait()
    loads["qr"].wait()
    loads["wv"].start()
    for head in range(HERE):
        pair, side = head // 2, (head % 2) * Q
        part = lax.dot_general(
            wk[:, head * DH : (head + 1) * DH], qn[:, head * DH : (head + 1) * DH],
            (((1,), (1,)), ((), ())), preferred_element_type=F32,
        )
        qt[pair, :DC, side : side + Q] = part.astype(BF16)
    for pair in range(PAIRS):
        turned = qr[:, pair * 2 * DR : (pair + 1) * 2 * DR].T
        qt[pair, DC : DC + DR, :Q] = turned[:DR]
        qt[pair, DC : DC + DR, Q:] = turned[DR:]

    lane = lax.broadcasted_iota(jnp.int32, (DR, ROWS), 1)
    row = lax.broadcasted_iota(jnp.int32, (DR, ROWS), 0)

    def prepare_new(slot):
        begin = NEWS[slot]
        ext[begin : begin + NEW, :] = jnp.concatenate(
            [nrope[slot], jnp.zeros((NEW, KEXT - DC - DR), BF16)], axis=1
        )

    def prepare_cached(slot):
        live = jnp.broadcast_to(lens[slot], (DR, ROWS))
        dead = jnp.where((row == 0) & (lane >= live), 1.0, 0.0).astype(BF16)
        wide = jnp.concatenate([rope[slot], dead], axis=0).T
        for begin, first, count in SLOT_ROWS[slot]:
            ext[begin : begin + count, :] = wide[first : first + count]

    def turn(begin, count, column, columns):
        rows = lat[begin : begin + count, :]
        if columns > count:
            rows = jnp.concatenate([rows, jnp.zeros((columns - count, DC), BF16)], axis=0)
        latt[:, column : column + columns] = rows.T

    local_row = lax.broadcasted_iota(jnp.int32, (CTX * NEW, 2 * Q), 0)
    query = lax.rem(lax.broadcasted_iota(jnp.int32, (CTX * NEW, 2 * Q), 1), Q)
    slot_of = lax.div(local_row, NEW)
    owner = jnp.where(
        slot_of == 0, me, jnp.where(slot_of == 1, sib, jnp.where(slot_of == 2, par, far))
    )
    fresh = owner * NEW + lax.rem(local_row, NEW) <= query

    score, weight, factor = (score0, score1), (weight0, weight1), (factor0, factor1)
    items = [(chunk, pair) for chunk in range(len(CHUNKS)) for pair in range(PAIRS)]

    def score_of(index):
        chunk, pair = items[index]
        begin, count = CHUNKS[chunk][:2]
        keys = jnp.concatenate(
            [lat[begin : begin + count, :], ext[begin : begin + count, :]], axis=1
        )
        score[index % 2][:count] = jnp.dot(keys, qt[pair], preferred_element_type=F32)

    def weigh(index):
        chunk, pair = items[index]
        begin, count, _, columns = CHUNKS[chunk]
        scores = score[index % 2][:count]
        if begin in FRESH:
            lo, hi = FRESH[begin]
            new = hi - lo
            scores = jnp.concatenate(
                [jnp.where(fresh[lo:hi], scores[:new], BLOCKED), scores[new:]], axis=0
            )
        level = jnp.max(scores, axis=0, keepdims=True)
        if chunk:
            level = jnp.maximum(top[pair], level)
            change = jnp.exp2((top[pair] - level) * SCALE)
            factor[index % 2][...] = change
        weights = jnp.exp2((scores - level) * SCALE)
        sums = jnp.sum(weights, axis=0, keepdims=True)
        top[pair] = level
        total[pair] = total[pair] * change + sums if chunk else sums
        weights = weights.astype(BF16)
        if columns > count:
            weights = jnp.concatenate([weights, jnp.zeros((columns - count, 2 * Q), BF16)], axis=0)
        weight[index % 2][:columns] = weights

    def gather_in(index):
        chunk, pair = items[index]
        _, _, column, columns = CHUNKS[chunk]
        part = jnp.dot(
            latt[:, column : column + columns],
            weight[index % 2][:columns],
            preferred_element_type=F32,
        )
        acc[pair] = acc[pair] * factor[index % 2][...] + part if chunk else part

    def finish(index):
        pair = items[index][1]
        mean = (acc[pair] * (1.0 / total[pair])).astype(BF16)
        for side in range(2):
            head = 2 * pair + side
            out[0, :, head * DV : (head + 1) * DV] = lax.dot_general(
                mean[:, side * Q : (side + 1) * Q], wv[:, head * DV : (head + 1) * DV],
                (((0,), (0,)), ((), ())), preferred_element_type=F32,
            ).astype(BF16)

    def onward(indices):
        for k in indices:
            to_par[k].wait_recv()
            forward[k].start()

    def before_item(index):
        if index == 0:
            for name in ("cl", "cr", "nl", "nr", "ln"):
                loads[name].wait()
            prepare_new(0)
            prepare_cached(0)
            turn(*CHUNKS[0])
        if index == PAIRS - 1:
            for k in (2, 3, 5):
                to_par[k].start()
        if index == PAIRS:
            for copy in to_sib:
                copy.wait_recv()
            prepare_new(1)
            prepare_cached(1)
            turn(*CHUNKS[1])
        if index == 2 * PAIRS - 1:
            onward(range(2))
        if index == 2 * PAIRS:
            onward(range(4, 5))
            prepare_cached(2)
            turn(*CHUNKS[2])
        if index == 2 * PAIRS + 2:
            pl.semaphore_wait(ready, 1)
            to_par[6].start()
            to_far.start()
        if index == 3 * PAIRS:
            onward((2, 3, 5))
            for k in (0, 1, 4):
                forward[k].wait_recv()
            prepare_new(2)
            prepare_cached(3)
            turn(*CHUNKS[3])
        if index == 4 * PAIRS:
            loads["wv"].wait()
            for k in (2, 3, 5):
                forward[k].wait_recv()
            to_par[6].wait_recv()
            to_far.wait_recv()
            prepare_new(3)
            turn(*CHUNKS[4])

    stages = (score_of, weigh, gather_in)
    done = [0, 0, 0]

    def advance(stage, index):
        if done[stage] <= index < len(items):
            assert done[stage] == index
            done[stage] += 1
            stages[stage](index)

    last = len(items) - PAIRS
    for index in range(len(items) + 3):
        if index in (2 * PAIRS, 3 * PAIRS, 4 * PAIRS):
            advance(1, index - 1)
            advance(2, index - 2)
            advance(2, index - 1)
        before_item(index)
        advance(0, index)
        if index >= 1:
            advance(1, index - 1)
        if index >= 2:
            advance(2, index - 2)
        if index >= last + 3:
            finish(index - 3)
    for copy in to_par + to_sib + forward + [to_far]:
        copy.wait_send()


def shards(*operands):
    operands = operands[:3] + (jnp.swapaxes(operands[3], 1, 2),) + operands[4:]
    operands = tuple(
        x if index == 6 else pltpu.with_memory_space_constraint(x, pltpu.HBM)
        for index, x in enumerate(operands)
    )
    return pl.pallas_call(
        kernel,
        out_shape=pltpu.VMEM((1, Q, HERE * DV), BF16),
        in_specs=[pl.BlockSpec(memory_space=pltpu.HBM)] * 9,
        out_specs=pl.BlockSpec(memory_space=pltpu.VMEM),
        scratch_shapes=[
            pltpu.VMEM((Q, HERE * DH), BF16),
            pltpu.VMEM((Q, HERE * DR), BF16),
            pltpu.VMEM((DC, HERE * DH), BF16),
            pltpu.VMEM((DC, HERE * DV), BF16),
            pltpu.VMEM((NROW, DC), BF16),
            pltpu.VMEM((CTX, DR, ROWS), BF16),
            pltpu.VMEM((CTX, NEW, DR), BF16),
            pltpu.VMEM((CTX, 1, 1), jnp.int32),
            pltpu.VMEM((NROW, KEXT - DC), BF16),
            pltpu.VMEM((DC, TURNED), BF16),
            pltpu.VMEM((PAIRS, KEXT, 2 * Q), BF16),
            pltpu.VMEM((PAIRS, DC, 2 * Q), F32),
            pltpu.VMEM((PAIRS, 1, 2 * Q), F32),
            pltpu.VMEM((PAIRS, 1, 2 * Q), F32),
            pltpu.VMEM((2 * ROWS, 2 * Q), F32),
            pltpu.VMEM((2 * ROWS, 2 * Q), F32),
            pltpu.VMEM((2 * ROWS, 2 * Q), BF16),
            pltpu.VMEM((2 * ROWS, 2 * Q), BF16),
            pltpu.VMEM((1, 2 * Q), F32),
            pltpu.VMEM((1, 2 * Q), F32),
            pltpu.SemaphoreType.DMA((9,)),
        ]
        + [pltpu.SemaphoreType.DMA((7,))] * 6
        + [pltpu.SemaphoreType.DMA((1,))] * 2
        + [pltpu.SemaphoreType.REGULAR],
        compiler_params=pltpu.CompilerParams(
            collective_id=0, has_side_effects=True, vmem_limit_bytes=40 << 20
        ),
        cost_estimate=pl.CostEstimate(
            flops=7_000_000_000, bytes_accessed=7_000_000, transcendentals=2_400_000
        ),
        name="latent_attention",
    )(*operands)


def solution(mesh):
    return jax.shard_map(
        shards,
        mesh=mesh,
        in_specs=(
            P("req", None, None),
            P("req", None, None),
            P("req", "ctx", None),
            P("req", "ctx", None),
            P("req", "ctx", None),
            P("req", "ctx", None),
            P("req", "ctx"),
            P(None, "ctx"),
            P(None, "ctx"),
        ),
        out_specs=P("req", None, "ctx"),
        check_vma=False,
    )
```

```python
import functools
import math

import jax
import jax.numpy as jnp
from jax import lax
from jax.experimental import pallas as pl
from jax.experimental.pallas import tpu as pltpu
from jax.sharding import PartitionSpec as P

DC = 512
DR = 64
DH = 128
DV = 128
HEADS = 64
CTX = 4
HERE = HEADS // CTX
PAIRS = HERE // 2
Q = 128
ROWS = 256
NEW = 32
NROW = CTX * (ROWS + NEW)
KEXT = DC + 128
LOG2E = 1.4426950408889634
SCALE = LOG2E / math.sqrt(DH + DR)
BLOCKED = -1e30
MESH = pl.DeviceIdType.MESH
F32 = jnp.float32
BF16 = jnp.bfloat16

PIECES = (128, 80, 48)
STARTS = (0, 128, 208)
RELAYED = 2
NEAR0 = 2 * ROWS
FAR0 = NEAR0 + 2 * NEW + PIECES[0]
LAST0 = FAR0 + NEW + PIECES[0] + PIECES[1]
NEWS = (NEAR0, NEAR0 + NEW, FAR0, LAST0)
LANDS = (
    None,
    (ROWS,),
    (NEAR0 + 2 * NEW, LAST0 - PIECES[1], LAST0 + NEW + PIECES[1]),
    (FAR0 + NEW, LAST0 + NEW, LAST0 + NEW + PIECES[1] + PIECES[2]),
)
FRESH = {NEAR0: (0, 2 * NEW), FAR0: (2 * NEW, 3 * NEW), LAST0: (3 * NEW, 4 * NEW)}
SLOT_ROWS = (
    ((0, 0, ROWS),),
    ((ROWS, 0, ROWS),),
    tuple(zip(LANDS[2], STARTS, PIECES)),
    tuple(zip(LANDS[3], STARTS, PIECES)),
)
CHUNKS = (
    (0, ROWS, 0, ROWS),
    (ROWS, ROWS, ROWS, ROWS),
    (NEAR0, FAR0 - NEAR0, 512, 256),
    (FAR0, LAST0 - FAR0, 768, 256),
    (LAST0, NROW - LAST0, 1024, 256),
)
TURNED = 1280


def kernel(
    qn_hbm, qr_hbm, cl_hbm, cr_hbm, nl_hbm, nr_hbm, len_hbm, wk_hbm, wv_hbm, out,
    qn, qr, wk, wv, lat, rope, nrope, lens, ext, latt, qt, acc, top, total,
    score0, score1, weight0, weight1, factor0, factor1,
    load_sem, sib_send, sib_recv, par_send, par_recv, fwd_send, fwd_recv, far_send, far_recv, ready,
):
    me = lax.axis_index("ctx")
    sib = me + 1 - 2 * lax.rem(me, 2)
    par = lax.rem(me + 2, CTX)
    far = lax.rem(sib + 2, CTX)

    def local(index, src, dst):
        return pltpu.make_async_copy(src, dst, load_sem.at[index])

    loads = dict(
        wk=local(0, wk_hbm, wk),
        qn=local(1, qn_hbm.at[0, :, pl.ds(pl.multiple_of(me * HERE * DH, HERE * DH), HERE * DH)], qn),
        qr=local(2, qr_hbm.at[0, :, pl.ds(pl.multiple_of(me * HERE * DR, HERE * DR), HERE * DR)], qr),
        cl=local(3, cl_hbm.at[0], lat.at[pl.ds(0, ROWS)]),
        cr=local(4, cr_hbm.at[0], rope.at[0]),
        nl=local(5, nl_hbm.at[0], lat.at[pl.ds(NEWS[0], NEW)]),
        nr=local(6, nr_hbm.at[0], nrope.at[0]),
        ln=local(7, len_hbm, lens.at[0]),
        wv=local(8, wv_hbm, wv),
    )
    barrier = pltpu.get_barrier_semaphore()
    for peer in (sib, par):
        pl.semaphore_signal(barrier, inc=1, device_id={"ctx": peer}, device_id_type=MESH)
    for name in ("wk", "qn", "qr", "cl", "cr", "nl", "nr", "ln"):
        loads[name].start()
    pl.semaphore_wait(barrier, 2)
    pl.semaphore_signal(ready, inc=1, device_id={"ctx": sib}, device_id_type=MESH)

    def remote(src, dst, send, recv, index, peer):
        return pltpu.make_async_remote_copy(
            src_ref=src, dst_ref=dst, send_sem=send.at[index], recv_sem=recv.at[index],
            device_id={"ctx": peer}, device_id_type=MESH,
        )

    def small(slot):
        return (
            rope.at[slot], lens.at[slot], nrope.at[slot], lat.at[pl.ds(NEWS[slot], NEW)],
        )

    mine = (cr_hbm.at[0], len_hbm, nr_hbm.at[0], nl_hbm.at[0])
    pieces = tuple(cl_hbm.at[0, pl.ds(start, count)] for start, count in zip(STARTS, PIECES))

    def landed(slot):
        return tuple(lat.at[pl.ds(row, count)] for row, _, count in SLOT_ROWS[slot])

    to_par = [
        remote(src, dst, par_send, par_recv, k, par)
        for k, (src, dst) in enumerate(zip(mine + pieces, small(2) + landed(2)))
    ]
    to_sib = [
        remote(src, dst, sib_send, sib_recv, k, sib)
        for k, (src, dst) in enumerate(zip(mine + (cl_hbm.at[0],), small(1) + landed(1)))
    ]
    forward = [
        remote(src, dst, fwd_send, fwd_recv, k, sib)
        for k, (src, dst) in enumerate(zip(small(2) + landed(2)[:RELAYED], small(3) + landed(3)[:RELAYED]))
    ]
    to_far = remote(pieces[RELAYED], landed(3)[RELAYED], far_send, far_recv, 0, far)
    for copy in to_par[:2] + to_par[4:5] + to_sib:
        copy.start()

    row_of = lax.broadcasted_iota(jnp.int32, (KEXT - DC - DR, 2 * Q), 0)
    tail = jnp.where(row_of == 0, BLOCKED, 0.0).astype(BF16)
    for pair in range(PAIRS):
        qt[pair, DC + DR :, :] = tail

    loads["wk"].wait()
    loads["qn"].wait()
    loads["qr"].wait()
    loads["wv"].start()
    for head in range(HERE):
        pair, side = head // 2, (head % 2) * Q
        part = lax.dot_general(
            wk[:, head * DH : (head + 1) * DH], qn[:, head * DH : (head + 1) * DH],
            (((1,), (1,)), ((), ())), preferred_element_type=F32,
        )
        qt[pair, :DC, side : side + Q] = part.astype(BF16)
    for pair in range(PAIRS):
        turned = qr[:, pair * 2 * DR : (pair + 1) * 2 * DR].T
        qt[pair, DC : DC + DR, :Q] = turned[:DR]
        qt[pair, DC : DC + DR, Q:] = turned[DR:]

    lane = lax.broadcasted_iota(jnp.int32, (DR, ROWS), 1)
    row = lax.broadcasted_iota(jnp.int32, (DR, ROWS), 0)

    def prepare_new(slot):
        begin = NEWS[slot]
        ext[begin : begin + NEW, :] = jnp.concatenate(
            [nrope[slot], jnp.zeros((NEW, KEXT - DC - DR), BF16)], axis=1
        )

    def prepare_cached(slot):
        live = jnp.broadcast_to(lens[slot], (DR, ROWS))
        dead = jnp.where((row == 0) & (lane >= live), 1.0, 0.0).astype(BF16)
        wide = jnp.concatenate([rope[slot], dead], axis=0).T
        for begin, first, count in SLOT_ROWS[slot]:
            ext[begin : begin + count, :] = wide[first : first + count]

    def turn(begin, count, column, columns):
        rows = lat[begin : begin + count, :]
        if columns > count:
            rows = jnp.concatenate([rows, jnp.zeros((columns - count, DC), BF16)], axis=0)
        latt[:, column : column + columns] = rows.T

    local_row = lax.broadcasted_iota(jnp.int32, (CTX * NEW, 2 * Q), 0)
    query = lax.rem(lax.broadcasted_iota(jnp.int32, (CTX * NEW, 2 * Q), 1), Q)
    slot_of = lax.div(local_row, NEW)
    owner = jnp.where(
        slot_of == 0, me, jnp.where(slot_of == 1, sib, jnp.where(slot_of == 2, par, far))
    )
    fresh = owner * NEW + lax.rem(local_row, NEW) <= query

    score, weight, factor = (score0, score1), (weight0, weight1), (factor0, factor1)
    items = [(chunk, pair) for chunk in range(len(CHUNKS)) for pair in range(PAIRS)]

    def score_of(index):
        chunk, pair = items[index]
        begin, count = CHUNKS[chunk][:2]
        keys = jnp.concatenate(
            [lat[begin : begin + count, :], ext[begin : begin + count, :]], axis=1
        )
        score[index % 2][:count] = jnp.dot(keys, qt[pair], preferred_element_type=F32)

    def weigh(index):
        chunk, pair = items[index]
        begin, count, _, columns = CHUNKS[chunk]
        scores = score[index % 2][:count]
        if begin in FRESH:
            lo, hi = FRESH[begin]
            new = hi - lo
            scores = jnp.concatenate(
                [jnp.where(fresh[lo:hi], scores[:new], BLOCKED), scores[new:]], axis=0
            )
        level = jnp.max(scores, axis=0, keepdims=True)
        if chunk:
            level = jnp.maximum(top[pair], level)
            change = jnp.exp2((top[pair] - level) * SCALE)
            factor[index % 2][...] = change
        weights = jnp.exp2((scores - level) * SCALE)
        sums = jnp.sum(weights, axis=0, keepdims=True)
        top[pair] = level
        total[pair] = total[pair] * change + sums if chunk else sums
        weights = weights.astype(BF16)
        if columns > count:
            weights = jnp.concatenate([weights, jnp.zeros((columns - count, 2 * Q), BF16)], axis=0)
        weight[index % 2][:columns] = weights

    def gather_in(index):
        chunk, pair = items[index]
        _, _, column, columns = CHUNKS[chunk]
        part = jnp.dot(
            latt[:, column : column + columns],
            weight[index % 2][:columns],
            preferred_element_type=F32,
        )
        acc[pair] = acc[pair] * factor[index % 2][...] + part if chunk else part

    def finish(index):
        pair = items[index][1]
        mean = (acc[pair] * (1.0 / total[pair])).astype(BF16)
        for side in range(2):
            head = 2 * pair + side
            out[0, :, head * DV : (head + 1) * DV] = lax.dot_general(
                mean[:, side * Q : (side + 1) * Q], wv[:, head * DV : (head + 1) * DV],
                (((0,), (0,)), ((), ())), preferred_element_type=F32,
            ).astype(BF16)

    def onward(indices):
        for k in indices:
            to_par[k].wait_recv()
            forward[k].start()

    def before_item(index):
        if index == 0:
            for name in ("cl", "cr", "nl", "nr", "ln"):
                loads[name].wait()
            prepare_new(0)
            prepare_cached(0)
            turn(*CHUNKS[0])
        if index == PAIRS - 1:
            for k in (2, 3, 5):
                to_par[k].start()
        if index == PAIRS:
            for copy in to_sib:
                copy.wait_recv()
            prepare_new(1)
            prepare_cached(1)
            turn(*CHUNKS[1])
        if index == 2 * PAIRS - 1:
            onward(range(2))
        if index == 2 * PAIRS:
            onward(range(4, 5))
            pl.semaphore_wait(ready, 1)
            to_par[6].start()
            to_far.start()
            prepare_cached(2)
            turn(*CHUNKS[2])
        if index == 3 * PAIRS:
            onward((2, 3, 5))
            for k in (0, 1, 4):
                forward[k].wait_recv()
            prepare_new(2)
            prepare_cached(3)
            turn(*CHUNKS[3])
        if index == 4 * PAIRS:
            loads["wv"].wait()
            for k in (2, 3, 5):
                forward[k].wait_recv()
            to_par[6].wait_recv()
            to_far.wait_recv()
            prepare_new(3)
            turn(*CHUNKS[4])

    stages = (score_of, weigh, gather_in)
    done = [0, 0, 0]

    def advance(stage, index):
        if done[stage] <= index < len(items):
            assert done[stage] == index
            done[stage] += 1
            stages[stage](index)

    last = len(items) - PAIRS
    for index in range(len(items) + 3):
        if index in (2 * PAIRS, 3 * PAIRS):
            advance(1, index - 1)
            advance(2, index - 2)
            advance(2, index - 1)
        before_item(index)
        advance(0, index)
        if index >= 1:
            advance(1, index - 1)
        if index >= 2:
            advance(2, index - 2)
        if index >= last + 3:
            finish(index - 3)
    for copy in to_par + to_sib + forward + [to_far]:
        copy.wait_send()


def shards(*operands):
    operands = operands[:3] + (jnp.swapaxes(operands[3], 1, 2),) + operands[4:]
    operands = tuple(
        x if index == 6 else pltpu.with_memory_space_constraint(x, pltpu.HBM)
        for index, x in enumerate(operands)
    )
    return pl.pallas_call(
        kernel,
        out_shape=pltpu.VMEM((1, Q, HERE * DV), BF16),
        in_specs=[pl.BlockSpec(memory_space=pltpu.HBM)] * 9,
        out_specs=pl.BlockSpec(memory_space=pltpu.VMEM),
        scratch_shapes=[
            pltpu.VMEM((Q, HERE * DH), BF16),
            pltpu.VMEM((Q, HERE * DR), BF16),
            pltpu.VMEM((DC, HERE * DH), BF16),
            pltpu.VMEM((DC, HERE * DV), BF16),
            pltpu.VMEM((NROW, DC), BF16),
            pltpu.VMEM((CTX, DR, ROWS), BF16),
            pltpu.VMEM((CTX, NEW, DR), BF16),
            pltpu.VMEM((CTX, 1, 1), jnp.int32),
            pltpu.VMEM((NROW, KEXT - DC), BF16),
            pltpu.VMEM((DC, TURNED), BF16),
            pltpu.VMEM((PAIRS, KEXT, 2 * Q), BF16),
            pltpu.VMEM((PAIRS, DC, 2 * Q), F32),
            pltpu.VMEM((PAIRS, 1, 2 * Q), F32),
            pltpu.VMEM((PAIRS, 1, 2 * Q), F32),
            pltpu.VMEM((2 * ROWS, 2 * Q), F32),
            pltpu.VMEM((2 * ROWS, 2 * Q), F32),
            pltpu.VMEM((2 * ROWS, 2 * Q), BF16),
            pltpu.VMEM((2 * ROWS, 2 * Q), BF16),
            pltpu.VMEM((1, 2 * Q), F32),
            pltpu.VMEM((1, 2 * Q), F32),
            pltpu.SemaphoreType.DMA((9,)),
        ]
        + [pltpu.SemaphoreType.DMA((7,))] * 6
        + [pltpu.SemaphoreType.DMA((1,))] * 2
        + [pltpu.SemaphoreType.REGULAR],
        compiler_params=pltpu.CompilerParams(
            collective_id=0, has_side_effects=True, vmem_limit_bytes=40 << 20
        ),
        cost_estimate=pl.CostEstimate(
            flops=7_000_000_000, bytes_accessed=7_000_000, transcendentals=2_400_000
        ),
        name="latent_attention",
    )(*operands)


def solution(mesh):
    return jax.shard_map(
        shards,
        mesh=mesh,
        in_specs=(
            P("req", None, None),
            P("req", None, None),
            P("req", "ctx", None),
            P("req", "ctx", None),
            P("req", "ctx", None),
            P("req", "ctx", None),
            P("req", "ctx"),
            P(None, "ctx"),
            P(None, "ctx"),
        ),
        out_specs=P("req", None, "ctx"),
        check_vma=False,
    )
```

```python
import functools
import math

import jax
import jax.numpy as jnp
from jax import lax
from jax.experimental import pallas as pl
from jax.experimental.pallas import tpu as pltpu
from jax.sharding import PartitionSpec as P

DC = 512
DR = 64
DH = 128
DV = 128
HEADS = 64
CTX = 4
HERE = HEADS // CTX
PAIRS = HERE // 2
Q = 128
ROWS = 256
NEW = 32
NROW = CTX * (ROWS + NEW)
KEXT = DC + 128
LOG2E = 1.4426950408889634
SCALE = LOG2E / math.sqrt(DH + DR)
BLOCKED = -1e30
MESH = pl.DeviceIdType.MESH
F32 = jnp.float32
BF16 = jnp.bfloat16

PIECES = (128, 80, 48)
STARTS = (0, 128, 208)
RELAYED = 2
NEAR0 = 2 * ROWS
FAR0 = NEAR0 + 2 * NEW + PIECES[0]
LAST0 = FAR0 + NEW + PIECES[0] + PIECES[1]
NEWS = (NEAR0, NEAR0 + NEW, FAR0, LAST0)
LANDS = (
    None,
    (ROWS,),
    (NEAR0 + 2 * NEW, LAST0 - PIECES[1], LAST0 + NEW + PIECES[1]),
    (FAR0 + NEW, LAST0 + NEW, LAST0 + NEW + PIECES[1] + PIECES[2]),
)
FRESH = {NEAR0: (0, 2 * NEW), FAR0: (2 * NEW, 3 * NEW), LAST0: (3 * NEW, 4 * NEW)}
SLOT_ROWS = (
    ((0, 0, ROWS),),
    ((ROWS, 0, ROWS),),
    tuple(zip(LANDS[2], STARTS, PIECES)),
    tuple(zip(LANDS[3], STARTS, PIECES)),
)
CHUNKS = (
    (0, ROWS, 0, ROWS),
    (ROWS, ROWS, ROWS, ROWS),
    (NEAR0, FAR0 - NEAR0, 512, 256),
    (FAR0, LAST0 - FAR0, 768, 256),
    (LAST0, NROW - LAST0, 1024, 256),
)
TURNED = 1280


def kernel(
    qn_hbm, qr_hbm, cl_hbm, cr_hbm, nl_hbm, nr_hbm, len_hbm, wk_hbm, wv_hbm, out,
    qn, qr, wk, wv, lat, rope, nrope, lens, ext, latt, qt, acc, top, total,
    score0, score1, weight0, weight1, factor0, factor1,
    load_sem, sib_send, sib_recv, par_send, par_recv, fwd_send, fwd_recv, far_send, far_recv, ready,
):
    me = lax.axis_index("ctx")
    sib = me + 1 - 2 * lax.rem(me, 2)
    par = lax.rem(me + 2, CTX)
    far = lax.rem(sib + 2, CTX)

    def local(index, src, dst):
        return pltpu.make_async_copy(src, dst, load_sem.at[index])

    loads = dict(
        qn=local(1, qn_hbm.at[0, :, pl.ds(pl.multiple_of(me * HERE * DH, HERE * DH), HERE * DH)], qn),
        qr=local(2, qr_hbm.at[0, :, pl.ds(pl.multiple_of(me * HERE * DR, HERE * DR), HERE * DR)], qr),
        cl=local(3, cl_hbm.at[0], lat.at[pl.ds(0, ROWS)]),
        cr=local(4, cr_hbm.at[0], rope.at[0]),
        nl=local(5, nl_hbm.at[0], lat.at[pl.ds(NEWS[0], NEW)]),
        nr=local(6, nr_hbm.at[0], nrope.at[0]),
        ln=local(7, len_hbm, lens.at[0]),
        wv=local(8, wv_hbm, wv),
    )
    part = HERE * DH // 4
    for k in range(4):
        columns = pl.ds(k * part, part)
        loads[k] = local(9 + k, wk_hbm.at[:, columns], wk.at[:, columns])
    barrier = pltpu.get_barrier_semaphore()
    for peer in (sib, par):
        pl.semaphore_signal(barrier, inc=1, device_id={"ctx": peer}, device_id_type=MESH)
    for name in ("qn", 0, 1, 2, 3, "qr", "cl", "cr", "nl", "nr", "ln"):
        loads[name].start()
    pl.semaphore_wait(barrier, 2)
    pl.semaphore_signal(ready, inc=1, device_id={"ctx": sib}, device_id_type=MESH)

    def remote(src, dst, send, recv, index, peer):
        return pltpu.make_async_remote_copy(
            src_ref=src, dst_ref=dst, send_sem=send.at[index], recv_sem=recv.at[index],
            device_id={"ctx": peer}, device_id_type=MESH,
        )

    def small(slot):
        return (
            rope.at[slot], lens.at[slot], nrope.at[slot], lat.at[pl.ds(NEWS[slot], NEW)],
        )

    mine = (cr_hbm.at[0], len_hbm, nr_hbm.at[0], nl_hbm.at[0])
    pieces = tuple(cl_hbm.at[0, pl.ds(start, count)] for start, count in zip(STARTS, PIECES))

    def landed(slot):
        return tuple(lat.at[pl.ds(row, count)] for row, _, count in SLOT_ROWS[slot])

    to_par = [
        remote(src, dst, par_send, par_recv, k, par)
        for k, (src, dst) in enumerate(zip(mine + pieces, small(2) + landed(2)))
    ]
    to_sib = [
        remote(src, dst, sib_send, sib_recv, k, sib)
        for k, (src, dst) in enumerate(zip(mine + (cl_hbm.at[0],), small(1) + landed(1)))
    ]
    forward = [
        remote(src, dst, fwd_send, fwd_recv, k, sib)
        for k, (src, dst) in enumerate(zip(small(2) + landed(2)[:RELAYED], small(3) + landed(3)[:RELAYED]))
    ]
    to_far = remote(pieces[RELAYED], landed(3)[RELAYED], far_send, far_recv, 0, far)
    for copy in to_par[:2] + to_par[4:5] + to_sib:
        copy.start()

    row_of = lax.broadcasted_iota(jnp.int32, (KEXT - DC - DR, 2 * Q), 0)
    tail = jnp.where(row_of == 0, BLOCKED, 0.0).astype(BF16)
    for pair in range(PAIRS):
        qt[pair, DC + DR :, :] = tail

    loads["qn"].wait()
    loads["wv"].start()
    for head in range(HERE):
        if head % (HERE // 4) == 0:
            loads[head // (HERE // 4)].wait()
        pair, side = head // 2, (head % 2) * Q
        part = lax.dot_general(
            wk[:, head * DH : (head + 1) * DH], qn[:, head * DH : (head + 1) * DH],
            (((1,), (1,)), ((), ())), preferred_element_type=F32,
        )
        qt[pair, :DC, side : side + Q] = part.astype(BF16)
    loads["qr"].wait()
    for pair in range(PAIRS):
        turned = qr[:, pair * 2 * DR : (pair + 1) * 2 * DR].T
        qt[pair, DC : DC + DR, :Q] = turned[:DR]
        qt[pair, DC : DC + DR, Q:] = turned[DR:]

    lane = lax.broadcasted_iota(jnp.int32, (DR, ROWS), 1)
    row = lax.broadcasted_iota(jnp.int32, (DR, ROWS), 0)

    def prepare_new(slot):
        begin = NEWS[slot]
        ext[begin : begin + NEW, :] = jnp.concatenate(
            [nrope[slot], jnp.zeros((NEW, KEXT - DC - DR), BF16)], axis=1
        )

    def prepare_cached(slot):
        live = jnp.broadcast_to(lens[slot], (DR, ROWS))
        dead = jnp.where((row == 0) & (lane >= live), 1.0, 0.0).astype(BF16)
        wide = jnp.concatenate([rope[slot], dead], axis=0).T
        for begin, first, count in SLOT_ROWS[slot]:
            ext[begin : begin + count, :] = wide[first : first + count]

    def turn(begin, count, column, columns):
        rows = lat[begin : begin + count, :]
        if columns > count:
            rows = jnp.concatenate([rows, jnp.zeros((columns - count, DC), BF16)], axis=0)
        latt[:, column : column + columns] = rows.T

    local_row = lax.broadcasted_iota(jnp.int32, (CTX * NEW, 2 * Q), 0)
    query = lax.rem(lax.broadcasted_iota(jnp.int32, (CTX * NEW, 2 * Q), 1), Q)
    slot_of = lax.div(local_row, NEW)
    owner = jnp.where(
        slot_of == 0, me, jnp.where(slot_of == 1, sib, jnp.where(slot_of == 2, par, far))
    )
    fresh = owner * NEW + lax.rem(local_row, NEW) <= query

    score, weight, factor = (score0, score1), (weight0, weight1), (factor0, factor1)
    items = [(chunk, pair) for chunk in range(len(CHUNKS)) for pair in range(PAIRS)]

    def score_of(index):
        chunk, pair = items[index]
        begin, count = CHUNKS[chunk][:2]
        keys = jnp.concatenate(
            [lat[begin : begin + count, :], ext[begin : begin + count, :]], axis=1
        )
        score[index % 2][:count] = jnp.dot(keys, qt[pair], preferred_element_type=F32)

    def weigh(index):
        chunk, pair = items[index]
        begin, count, _, columns = CHUNKS[chunk]
        scores = score[index % 2][:count]
        if begin in FRESH:
            lo, hi = FRESH[begin]
            new = hi - lo
            scores = jnp.concatenate(
                [jnp.where(fresh[lo:hi], scores[:new], BLOCKED), scores[new:]], axis=0
            )
        level = jnp.max(scores, axis=0, keepdims=True)
        if chunk:
            level = jnp.maximum(top[pair], level)
            change = jnp.exp2((top[pair] - level) * SCALE)
            factor[index % 2][...] = change
        weights = jnp.exp2((scores - level) * SCALE)
        sums = jnp.sum(weights, axis=0, keepdims=True)
        top[pair] = level
        total[pair] = total[pair] * change + sums if chunk else sums
        weights = weights.astype(BF16)
        if columns > count:
            weights = jnp.concatenate([weights, jnp.zeros((columns - count, 2 * Q), BF16)], axis=0)
        weight[index % 2][:columns] = weights

    def gather_in(index):
        chunk, pair = items[index]
        _, _, column, columns = CHUNKS[chunk]
        part = jnp.dot(
            latt[:, column : column + columns],
            weight[index % 2][:columns],
            preferred_element_type=F32,
        )
        acc[pair] = acc[pair] * factor[index % 2][...] + part if chunk else part

    def finish(index):
        pair = items[index][1]
        mean = (acc[pair] * (1.0 / total[pair])).astype(BF16)
        for side in range(2):
            head = 2 * pair + side
            out[0, :, head * DV : (head + 1) * DV] = lax.dot_general(
                mean[:, side * Q : (side + 1) * Q], wv[:, head * DV : (head + 1) * DV],
                (((0,), (0,)), ((), ())), preferred_element_type=F32,
            ).astype(BF16)

    def onward(indices):
        for k in indices:
            to_par[k].wait_recv()
            forward[k].start()

    def before_item(index):
        if index == 0:
            for name in ("cl", "cr", "nl", "nr", "ln"):
                loads[name].wait()
            prepare_new(0)
            prepare_cached(0)
            turn(*CHUNKS[0])
        if index == PAIRS - 1:
            for k in (2, 3, 5):
                to_par[k].start()
        if index == PAIRS:
            for copy in to_sib:
                copy.wait_recv()
            prepare_new(1)
            prepare_cached(1)
            turn(*CHUNKS[1])
        if index == 2 * PAIRS - 1:
            pl.semaphore_wait(ready, 1)
            to_par[6].start()
            to_far.start()
            onward(range(2))
        if index == 2 * PAIRS:
            onward(range(4, 5))
            prepare_cached(2)
            turn(*CHUNKS[2])
        if index == 3 * PAIRS:
            onward((2, 3, 5))
            for k in (0, 1, 4):
                forward[k].wait_recv()
            prepare_new(2)
            prepare_cached(3)
            turn(*CHUNKS[3])
        if index == 4 * PAIRS:
            loads["wv"].wait()
            for k in (2, 3, 5):
                forward[k].wait_recv()
            to_par[6].wait_recv()
            to_far.wait_recv()
            prepare_new(3)
            turn(*CHUNKS[4])

    stages = (score_of, weigh, gather_in)
    done = [0, 0, 0]

    def advance(stage, index):
        if done[stage] <= index < len(items):
            assert done[stage] == index
            done[stage] += 1
            stages[stage](index)

    last = len(items) - PAIRS
    for index in range(len(items) + 3):
        if index in (2 * PAIRS, 3 * PAIRS):
            advance(1, index - 1)
            advance(2, index - 2)
            advance(2, index - 1)
        before_item(index)
        advance(0, index)
        if index >= 1:
            advance(1, index - 1)
        if index >= 2:
            advance(2, index - 2)
        if index >= last + 3:
            finish(index - 3)
    for copy in to_par + to_sib + forward + [to_far]:
        copy.wait_send()


def shards(*operands):
    operands = operands[:3] + (jnp.swapaxes(operands[3], 1, 2),) + operands[4:]
    operands = tuple(
        x if index == 6 else pltpu.with_memory_space_constraint(x, pltpu.HBM)
        for index, x in enumerate(operands)
    )
    return pl.pallas_call(
        kernel,
        out_shape=pltpu.VMEM((1, Q, HERE * DV), BF16),
        in_specs=[pl.BlockSpec(memory_space=pltpu.HBM)] * 9,
        out_specs=pl.BlockSpec(memory_space=pltpu.VMEM),
        scratch_shapes=[
            pltpu.VMEM((Q, HERE * DH), BF16),
            pltpu.VMEM((Q, HERE * DR), BF16),
            pltpu.VMEM((DC, HERE * DH), BF16),
            pltpu.VMEM((DC, HERE * DV), BF16),
            pltpu.VMEM((NROW, DC), BF16),
            pltpu.VMEM((CTX, DR, ROWS), BF16),
            pltpu.VMEM((CTX, NEW, DR), BF16),
            pltpu.VMEM((CTX, 1, 1), jnp.int32),
            pltpu.VMEM((NROW, KEXT - DC), BF16),
            pltpu.VMEM((DC, TURNED), BF16),
            pltpu.VMEM((PAIRS, KEXT, 2 * Q), BF16),
            pltpu.VMEM((PAIRS, DC, 2 * Q), F32),
            pltpu.VMEM((PAIRS, 1, 2 * Q), F32),
            pltpu.VMEM((PAIRS, 1, 2 * Q), F32),
            pltpu.VMEM((2 * ROWS, 2 * Q), F32),
            pltpu.VMEM((2 * ROWS, 2 * Q), F32),
            pltpu.VMEM((2 * ROWS, 2 * Q), BF16),
            pltpu.VMEM((2 * ROWS, 2 * Q), BF16),
            pltpu.VMEM((1, 2 * Q), F32),
            pltpu.VMEM((1, 2 * Q), F32),
            pltpu.SemaphoreType.DMA((13,)),
        ]
        + [pltpu.SemaphoreType.DMA((7,))] * 6
        + [pltpu.SemaphoreType.DMA((1,))] * 2
        + [pltpu.SemaphoreType.REGULAR],
        compiler_params=pltpu.CompilerParams(
            collective_id=0, has_side_effects=True, vmem_limit_bytes=40 << 20
        ),
        cost_estimate=pl.CostEstimate(
            flops=7_000_000_000, bytes_accessed=7_000_000, transcendentals=2_400_000
        ),
        name="latent_attention",
    )(*operands)


def solution(mesh):
    return jax.shard_map(
        shards,
        mesh=mesh,
        in_specs=(
            P("req", None, None),
            P("req", None, None),
            P("req", "ctx", None),
            P("req", "ctx", None),
            P("req", "ctx", None),
            P("req", "ctx", None),
            P("req", "ctx"),
            P(None, "ctx"),
            P(None, "ctx"),
        ),
        out_specs=P("req", None, "ctx"),
        check_vma=False,
    )
```
